32 devices in a mesh: groups: 2 (over x), seq: 16 (over z, y, core).
Axes of the slice: x: 2, y: 2, z: 4, core: 2. Of those that a mesh axis runs over, the one named last changes fastest.
Arguments:
- queries: bfloat16 [24576, 2048], P(('groups', 'seq')), parts along dimension 0, may hold values from -6 to 6
- keys: bfloat16 [24576, 2048], P(('groups', 'seq')), parts along dimension 0, may hold values from -6 to 6
- values: bfloat16 [24576, 2048], P(('groups', 'seq')), parts along dimension 0, may hold values from -6 to 6
- memory_ids: int32 [384, 2], P(('groups', 'seq')), parts along dimension 0, may hold values from 0 to 7, all different within a row
- gate_levels: int32 [384, 2], P(('groups', 'seq')), parts along dimension 0, may hold values from 1 to 15
- norm_gain: float32 [2048], replicated, may hold values from 0.1 to 1.9
Outputs:
- normed: bfloat16 [24576, 2048], P(('groups', 'seq')), parts along dimension 0
The draws below stay inside these ranges and needn't reach their ends.
There are 2 independent parts, one for each index of `groups`. The reference program is written for one: setup_inputs(seed, part) draws one part's arguments, and reference() takes and returns one part's arrays. A program takes and returns all parts, laid end to end along the dimension named above; an argument that names none is the same for every part. Nothing has to cross between parts.
Inputs may be any that keep to these rules, and one draw needn't show every extreme that they name: `memory_ids`: the 2 memories of a block differ, and every memory is named by some block.
All inputs are finite; a program needn't handle non-finite values.
Results may differ from the reference program's by a relative error of at most 0.005.
Values may be sent and summed in bfloat16 or wider, within the bound.
A program may use at most 128 MiB of HBM per device.

```python
import jax
import jax.numpy as jnp
from jax import lax

HEADS = 16
HDIM = 128
MEMS = 8
TOPM = 2
BLOCK = 64
GATE_DEN = 16
TOK_DEV = 768
TOKENS = 12288
NBLK = 192
N_SEQ = 16


def with_ends(drawn, own_key, low, top_value):
    shape = drawn.shape
    place = [jax.random.randint(jax.random.fold_in(own_key, axis), (), 0, shape[axis]) for axis in range(len(shape))]
    drawn = drawn.at[tuple(place)].set(low)
    longest = shape.index(max(shape))
    place[longest] = (place[longest] + 1) % shape[longest]
    return drawn.at[tuple(place)].set(top_value)


def steps_of(stream_key, dims, shards, least, high):
    loudness, own = 1.0, jax.random.fold_in(stream_key, 6)
    for dim, shards_of in shards:
        heights = jnp.exp(jax.random.uniform(jax.random.fold_in(own, dim), (shards_of,), jnp.float32, least / len(shards), high / len(shards)))
        loudness = loudness * jnp.repeat(heights, dims[dim] // shards_of).reshape([-1 if axis == dim else 1 for axis in range(len(dims))])
    return loudness


def different_ones(stream_key, rows, number_of, top, lift):
    sequence = jax.random.permutation(jax.random.fold_in(stream_key, 1), number_of)
    pull = sequence
    for power in range(3):
        pull = pull * pull // number_of
    pull = pull * lift // number_of
    lots = jax.random.randint(jax.random.fold_in(stream_key, 2), (rows, number_of), 0, 4096) + pull
    fixed_rows = jax.random.permutation(jax.random.fold_in(stream_key, 3), rows)[jnp.arange(number_of) % rows]
    lots = jnp.where(jnp.arange(rows)[:, None] == fixed_rows[None, :], 1 << 14, lots)
    score = lots * number_of + jnp.arange(number_of)
    return lax.top_k(score.astype(jnp.int32), top)[1].astype(jnp.int32)


def normal_values(key, shape, spread, most, pieces=(), kind=jnp.bfloat16):
    loudness = steps_of(key, shape, pieces, -0.22, 0.18) if pieces else 1.0
    entries = jax.random.normal(key, shape, jnp.float32) * spread * loudness
    return jnp.minimum(jnp.maximum(entries, -most), most).astype(kind)


def setup_inputs(seed: int = 0, part: int = 0) -> dict:
    key_list = jax.random.split(jax.random.key(seed), 7)
    part_splits = jax.random.split(jax.random.fold_in(key_list[6], part), 7)
    queries = normal_values(part_splits[0], (TOKENS, HEADS * HDIM), 1.0, 6.0, ((0, 16),))
    keys = normal_values(part_splits[1], (TOKENS, HEADS * HDIM), 1.0, 6.0, ((0, 16),))
    values = normal_values(part_splits[2], (TOKENS, HEADS * HDIM), 1.0, 6.0, ((0, 16),))
    memory_ids = different_ones(part_splits[3], NBLK, MEMS, TOPM, 4096)
    gate_levels = with_ends(jax.random.randint(part_splits[4], (NBLK, TOPM), 1, GATE_DEN), jax.random.fold_in(part_splits[4], 1), 1, GATE_DEN - 1).astype(jnp.int32)
    norm_gain = jnp.clip(1.0 + 0.18 * jax.random.normal(key_list[5], (HEADS * HDIM,), jnp.float32), 0.1, 1.9)
    return {"queries": queries, "keys": keys, "values": values, "memory_ids": memory_ids, "gate_levels": gate_levels, "norm_gain": norm_gain}


def reference(queries, keys, values, memory_ids, gate_levels, norm_gain):
    per_dev = TOK_DEV // BLOCK
    gates = gate_levels.astype(jnp.float32) / GATE_DEN
    members = jnp.arange(MEMS, dtype=jnp.int32)
    onehot = (memory_ids[:, :, None] == members[None, None, :]).astype(jnp.float32)
    block_weights = lax.optimization_barrier(jnp.sum(gates[:, :, None] * onehot, axis=1))
    key_groups = keys.reshape(N_SEQ, per_dev, BLOCK, HEADS, HDIM)
    value_groups = values.reshape(N_SEQ, per_dev, BLOCK, HEADS, HDIM)
    weight_groups = block_weights.reshape(N_SEQ, per_dev, MEMS)

    def accumulate(state, inputs):
        key_part, value_part, weight_part = inputs
        block_state = jnp.einsum('bthk,bthd->bhkd', key_part.astype(jnp.float32), value_part.astype(jnp.float32))
        added = jnp.einsum('bm,bhkd->mhkd', weight_part, block_state, precision=lax.Precision.HIGHEST)
        return (state + added, None)
    start_state = jnp.zeros((MEMS, HEADS, HDIM, HDIM), jnp.float32)
    state, unused = lax.scan(accumulate, start_state, (key_groups, value_groups, weight_groups))
    shared = state.astype(jnp.bfloat16)
    query_groups = queries.reshape(N_SEQ, per_dev, BLOCK, HEADS, HDIM)
    id_groups = memory_ids.reshape(N_SEQ, per_dev, TOPM)
    gate_groups = gates.reshape(N_SEQ, per_dev, TOPM)
    gain = norm_gain.reshape(HEADS, HDIM)

    def read_group(inputs):
        query_part, id_part, gate_part = inputs
        readout = jnp.zeros((per_dev, BLOCK, HEADS, HDIM), jnp.float32)
        for route in range(TOPM):
            chosen = jnp.take(shared, id_part[:, route], axis=0).astype(jnp.float32)
            product = jnp.einsum('bthk,bhkd->bthd', query_part.astype(jnp.float32), chosen)
            readout = readout + gate_part[:, route][:, None, None, None] * product
        mean_square = lax.optimization_barrier(jnp.mean(readout * readout, axis=-1, keepdims=True))
        result = readout * lax.rsqrt(mean_square + 1e-05) * gain
        return result.astype(jnp.bfloat16).reshape(per_dev * BLOCK, HEADS * HDIM)
    normed = lax.map(read_group, (query_groups, id_groups, gate_groups))
    return normed.reshape(TOKENS, HEADS * HDIM)
```

```python
import functools

import jax
import jax.numpy as jnp
from jax import lax
from jax.experimental import pallas as pl
from jax.experimental.pallas import tpu as pltpu
from jax.sharding import PartitionSpec as P

HEADS = 16
HDIM = 128
MEMS = 8
BLOCK = 64
GATE_DEN = 16
HALF = HEADS // 2
ROWS = MEMS * HDIM
GROUP = 12
LAG = 3
MESH = pl.DeviceIdType.MESH
TAGS = "rnfhi"
WAYS = "ysm"
PLANNED = 16
CHUNKS = (
    (0, 0, 2, "YM"),
    (1, 0, 2, "ZE"),
    (2, 0, 2, "YM"),
    (3, 0, 2, "YM"),
    (4, 0, 2, "ZE"),
    (5, 0, 2, "YM"),
    (6, 0, 2, "YM"),
    (7, 0, 2, "YM"),
)
ORDER_END = (
    (0, 0), (1, 0), (2, 0), (3, 0), (4, 0), (0, 1), (5, 0), (6, 0), (2, 1), (7, 0), (3, 1), (5, 1),
    (1, 3), (6, 1), (4, 3), (0, 6), (7, 1), (0, 7), (1, 4), (2, 6), (4, 4), (3, 6), (2, 7), (0, 8),
    (0, 10), (3, 7), (0, 11), (1, 5), (5, 6), (6, 6), (4, 5), (5, 7), (7, 6), (2, 8), (2, 10), (6,
    7), (2, 11), (3, 8), (3, 10), (1, 7), (3, 11), (4, 7), (7, 7), (5, 8), (5, 10), (1, 8), (1, 10),
    (5, 11), (1, 11), (4, 8), (4, 10), (6, 8), (6, 10), (4, 11), (7, 8), (7, 10), (6, 11), (7, 11),
)
ORDER_INNER = (
    (0, 0), (1, 0), (2, 0), (3, 0), (4, 0), (0, 1), (1, 1), (2, 1), (4, 1), (1, 2), (3, 1), (0, 2),
    (5, 0), (6, 0), (4, 2), (0, 3), (2, 2), (7, 0), (5, 1), (0, 5), (3, 2), (2, 3), (6, 1), (3, 3),
    (5, 2), (2, 5), (3, 5), (6, 2), (7, 1), (5, 3), (0, 8), (0, 10), (7, 2), (6, 3), (0, 11), (1,
    4), (5, 5), (4, 4), (7, 3), (2, 8), (2, 10), (1, 5), (6, 5), (2, 11), (3, 8), (3, 10), (1, 6),
    (4, 5), (3, 11), (4, 6), (7, 5), (5, 8), (5, 10), (1, 7), (1, 8), (1, 10), (5, 11), (1, 11), (4,
    7), (4, 8), (4, 10), (6, 8), (6, 10), (4, 11), (6, 11), (7, 8), (7, 10), (7, 11),
)


def kernel(
    n, tok, orders,
    q_hbm, k_hbm, v_hbm, ids, levels, gain,
    o_hbm,
    q_buf, k_buf, v_buf, o_buf, own_w, sib_w, kt, st, sbuf, rbuf,
    sh0, sh1, sh2, sh3, sh4, sh5, sh6, sh7, sh8, sh9, sh10, sh11, sh12, sh13, sh14, sh15,
    gain_buf, q_sem, k_sem, v_sem, o_sem, n_sem,
    xk_send, xk_recv, xv_send, xv_recv, xw_send, xw_recv,
    c_send, c_recv, r_send, r_recv, g_send, g_recv,
):
    sh = (sh0, sh1, sh2, sh3, sh4, sh5, sh6, sh7, sh8, sh9, sh10, sh11, sh12, sh13, sh14, sh15)
    group = lax.axis_index("groups")
    me = lax.axis_index("seq")
    core = me % 2
    sibling = me + 1 - 2 * core
    steps = len(orders[0])

    def bit(mask):
        return (me // mask) % 2

    def partner(mask):
        return (group, me + mask - 2 * mask * bit(mask))

    def cols(head):
        return pl.ds(pl.multiple_of(head * HDIM, HDIM), HDIM)

    def own_head(slot):
        return core * HALF + slot if slot < HALF else (1 - core) * HALF + slot - HALF

    loads = []
    for i in range(HALF):
        kc = pltpu.make_async_copy(k_hbm.at[:, cols(own_head(i))], k_buf.at[0, i], k_sem.at[i])
        vc = pltpu.make_async_copy(v_hbm.at[:, cols(own_head(i))], v_buf.at[0, i], v_sem.at[i])
        kc.start()
        vc.start()
        loads.append((kc, vc))

    gain_load = pltpu.make_async_copy(gain, gain_buf, n_sem.at[0])
    gain_load.start()

    barrier = pltpu.get_barrier_semaphore()
    masks = [1] + sorted(orders[0])
    for mask in masks:
        pl.semaphore_signal(barrier, inc=1, device_id=partner(mask), device_id_type=MESH)

    blocks = tok // BLOCK
    member = lax.broadcasted_iota(jnp.int32, (MEMS, 2 * BLOCK), 0)
    lane = lax.broadcasted_iota(jnp.int32, (MEMS, 2 * BLOCK), 1)
    for p in range(blocks // 2):
        w = []
        for b in (2 * p, 2 * p + 1):
            w.append(
                jnp.where(member == ids[0, b], levels[0, b], 0)
                + jnp.where(member == ids[1, b], levels[1, b], 0)
            )
        both = jnp.where(lane < BLOCK, w[0], w[1]).astype(jnp.float32) / GATE_DEN
        own_w[:, p * 2 * BLOCK : (p + 1) * 2 * BLOCK] = both

    gain_load.wait()
    pl.semaphore_wait(barrier, len(masks))

    xw = pltpu.make_async_remote_copy(
        own_w, sib_w, xw_send.at[0], xw_recv.at[0], device_id=(group, sibling), device_id_type=MESH
    )
    xw.start()
    swaps = []
    for i in range(HALF):
        other = (1 - core) * HALF + i
        kc = pltpu.make_async_remote_copy(
            k_hbm.at[:, cols(other)], k_buf.at[1, i], xk_send.at[i], xk_recv.at[i],
            device_id=(group, sibling), device_id_type=MESH,
        )
        vc = pltpu.make_async_remote_copy(
            v_hbm.at[:, cols(other)], v_buf.at[1, i], xv_send.at[i], xv_recv.at[i],
            device_id=(group, sibling), device_id_type=MESH,
        )
        kc.start()
        vc.start()
        swaps.append((kc, vc))
    q_loads = []
    for slot in range(HEADS):
        qc = pltpu.make_async_copy(q_hbm.at[:, cols(own_head(slot))], q_buf.at[slot], q_sem.at[slot])
        qc.start()
        q_loads.append(qc)

    def local_state(c):
        for copy in loads[c]:
            copy.wait()
        if c == 0:
            xw.wait_recv()
        for copy in swaps[c]:
            copy.wait_recv()
        kt[0] = k_buf[0, c].T
        kt[1] = k_buf[1, c].T

        def one(m, carry):
            own = kt[0] * own_w[pl.ds(m, 1), :].astype(jnp.bfloat16)
            sib = kt[1] * sib_w[pl.ds(m, 1), :].astype(jnp.bfloat16)
            total = jnp.dot(own, v_buf[0, c], preferred_element_type=jnp.float32)
            total += jnp.dot(sib, v_buf[1, c], preferred_element_type=jnp.float32)
            st[c, pl.ds(pl.multiple_of(m * HDIM, HDIM), HDIM), :] = total
            return carry

        lax.fori_loop(0, MEMS, one, 0, unroll=4)

    low = [0] * HALF
    lows = [[] for _ in range(HALF)]
    reduces = [[] for _ in range(HALF)]
    gathers = [dict() for _ in range(HALF)]

    def rows(start, size):
        return pl.ds(pl.multiple_of(start, size), size)

    def part(start, size):
        if size >= HDIM:
            return (pl.ds(start // HDIM, size // HDIM),)
        return (start // HDIM, rows(start % HDIM, size))

    def send_half(c, s):
        size = ROWS >> (s + 1)
        b = bit(orders[c][s])
        lows[c].append(low[c])
        away = rows(low[c] + (1 - b) * size, size)
        low[c] = low[c] + b * size
        sbuf[c, away, :] = st[c, away, :].astype(jnp.bfloat16)
        copy = pltpu.make_async_remote_copy(
            sbuf.at[c, away], rbuf.at[c, size : 2 * size],
            r_send.at[c, s], r_recv.at[c, s],
            device_id=partner(orders[c][s]), device_id_type=MESH,
        )
        copy.start()
        reduces[c].append(copy)

    def gather(c, s):
        size = ROWS >> (s + 1)
        b = bit(orders[c][s])
        have = part(lows[c][s] + b * size, size)
        copy = pltpu.make_async_remote_copy(
            sh[c].at[*have], sh[c].at[*have],
            g_send.at[c, s], g_recv.at[c, s],
            device_id=partner(orders[c][s]), device_id_type=MESH,
        )
        copy.start()
        gathers[c][s] = copy

    cores = {}
    outs = []

    def readout(slot):
        q_loads[slot].wait()
        head = own_head(slot)
        scale = gain_buf[pl.ds(head, 1), :]

        def one(g, carry):
            for b in range(GROUP):
                b = g * GROUP + b
                here = pl.ds(pl.multiple_of(b * BLOCK, BLOCK), BLOCK)
                pair = jnp.concatenate(
                    [
                        sh[slot][ids[r, b]]
                        for r in range(2)
                    ],
                    axis=1,
                )
                product = jnp.dot(q_buf[slot, here, :], pair, preferred_element_type=jnp.float32)
                gates = [levels[r, b].astype(jnp.float32) / GATE_DEN for r in range(2)]
                total = gates[0] * product[:, :HDIM] + gates[1] * product[:, HDIM:]
                square = jnp.mean(total * total, axis=-1, keepdims=True)
                result = total * lax.rsqrt(square + 1e-05) * scale
                o_buf[slot, here, :] = result.astype(jnp.bfloat16)
            return carry

        lax.fori_loop(0, blocks // GROUP, one, 0)
        copy = pltpu.make_async_copy(o_buf.at[slot], o_hbm.at[:, cols(head)], o_sem.at[slot])
        copy.start()
        outs.append(copy)

    def stage(c, k):
        if k == 0:
            local_state(c)
            send_half(c, 0)
        elif k <= steps:
            s = k - 1
            size = ROWS >> (s + 1)
            reduces[c][s].wait_recv()
            keep = rows(low[c], size)
            total = st[c, keep, :] + rbuf[c, size : 2 * size, :].astype(jnp.float32)
            if k < steps:
                st[c, keep, :] = total
                send_half(c, k)
            else:
                owned = total.astype(jnp.bfloat16)
                if size >= HDIM:
                    owned = owned.reshape(size // HDIM, HDIM, HDIM)
                sh[c][part(low[c], size)] = owned
                gather(c, steps - 1)
        elif k < 2 * steps:
            s = 2 * steps - k
            gathers[c][s].wait_recv()
            gather(c, s - 1)
        elif k == 2 * steps:
            gathers[c][0].wait_recv()
            copy = pltpu.make_async_remote_copy(
                sh[c], sh[HALF + c], c_send.at[c], c_recv.at[c],
                device_id=(group, sibling), device_id_type=MESH,
            )
            copy.start()
            cores[c] = copy
            readout(c)
        else:
            cores[c].wait_recv()
            readout(HALF + c)

    plan = [(c + LAG * k, -k, c) for c in range(HALF) for k in range(2 * steps + 2)]
    for _, k, c in sorted(plan):
        stage(c, -k)

    xw.wait_send()
    for i in range(HALF):
        swaps[i][0].wait_send()
        swaps[i][1].wait_send()
        cores[i].wait_send()
        for s in range(steps):
            reduces[i][s].wait_send()
            gathers[i][s].wait_send()
    for copy in outs:
        copy.wait()


def plan_kernel(
    tok, chunks, order_end, order_inner,
    q_hbm, k_hbm, v_hbm, ids, levels, gain,
    o_hbm,
    q_buf, k_buf, v_buf, o_buf, own_w, sib_w, kt, st, sbuf, ybuf, zbuf, mbuf,
    sh0, sh1, sh2, sh3, sh4, sh5, sh6, sh7, sh8, sh9, sh10, sh11, sh12, sh13, sh14, sh15,
    gain_buf, q_sem, k_sem, v_sem, o_sem, n_sem,
    xk_send, xk_recv, xv_send, xv_recv, xw_send, xw_recv,
    c_send, c_recv, p_send, p_recv,
):
    sh = (sh0, sh1, sh2, sh3, sh4, sh5, sh6, sh7, sh8, sh9, sh10, sh11, sh12, sh13, sh14, sh15)
    group = lax.axis_index("groups")
    me = lax.axis_index("seq")
    core = me % 2
    y = (me // 2) % 2
    z = me // 4
    high = z // 2
    inner = (z + high) % 2
    sibling = me + 1 - 2 * core
    towards = {
        "y": me + 2 - 4 * y,
        "s": me + 4 - 8 * (z % 2),
        "m": me + 4 * (3 - 2 * z),
    }

    def device(way):
        return (group, towards[way])

    def cols(head):
        return pl.ds(pl.multiple_of(head * HDIM, HDIM), HDIM)

    def own_head(slot):
        return core * HALF + slot if slot < HALF else (1 - core) * HALF + slot - HALF

    loads = []
    for i in range(HALF):
        kc = pltpu.make_async_copy(k_hbm.at[:, cols(own_head(i))], k_buf.at[0, i], k_sem.at[i])
        vc = pltpu.make_async_copy(v_hbm.at[:, cols(own_head(i))], v_buf.at[0, i], v_sem.at[i])
        kc.start()
        vc.start()
        loads.append((kc, vc))

    gain_load = pltpu.make_async_copy(gain, gain_buf, n_sem.at[0])
    gain_load.start()

    barrier = pltpu.get_barrier_semaphore()
    pl.semaphore_signal(barrier, inc=1, device_id=(group, sibling), device_id_type=MESH)
    pl.semaphore_signal(barrier, inc=1, device_id=device("y"), device_id_type=MESH)
    pl.semaphore_signal(barrier, inc=1, device_id=device("s"), device_id_type=MESH)

    @pl.when(inner == 1)
    def _():
        pl.semaphore_signal(barrier, inc=1, device_id=device("m"), device_id_type=MESH)

    blocks = tok // BLOCK
    member = lax.broadcasted_iota(jnp.int32, (MEMS, 2 * BLOCK), 0)
    lane = lax.broadcasted_iota(jnp.int32, (MEMS, 2 * BLOCK), 1)
    for p in range(blocks // 2):
        w = []
        for b in (2 * p, 2 * p + 1):
            w.append(
                jnp.where(member == ids[0, b], levels[0, b], 0)
                + jnp.where(member == ids[1, b], levels[1, b], 0)
            )
        both = jnp.where(lane < BLOCK, w[0], w[1]).astype(jnp.float32) / GATE_DEN
        own_w[:, p * 2 * BLOCK : (p + 1) * 2 * BLOCK] = both

    gain_load.wait()
    pl.semaphore_wait(barrier, 3 + inner)

    xw = pltpu.make_async_remote_copy(
        own_w, sib_w, xw_send.at[0], xw_recv.at[0], device_id=(group, sibling), device_id_type=MESH
    )
    xw.start()
    swaps = []
    for i in range(HALF):
        other = (1 - core) * HALF + i
        kc = pltpu.make_async_remote_copy(
            k_hbm.at[:, cols(other)], k_buf.at[1, i], xk_send.at[i], xk_recv.at[i],
            device_id=(group, sibling), device_id_type=MESH,
        )
        vc = pltpu.make_async_remote_copy(
            v_hbm.at[:, cols(other)], v_buf.at[1, i], xv_send.at[i], xv_recv.at[i],
            device_id=(group, sibling), device_id_type=MESH,
        )
        kc.start()
        vc.start()
        swaps.append((kc, vc))
    q_loads = []
    for slot in range(HEADS):
        qc = pltpu.make_async_copy(q_hbm.at[:, cols(own_head(slot))], q_buf.at[slot], q_sem.at[slot])
        qc.start()
        q_loads.append(qc)

    fetched = set()

    def fetch(c):
        if c in fetched:
            return
        for copy in loads[c]:
            copy.wait()
        if not fetched:
            xw.wait_recv()
        fetched.add(c)
        for copy in swaps[c]:
            copy.wait_recv()
        kt[0] = k_buf[0, c].T
        kt[1] = k_buf[1, c].T

    def local(c, first, count):
        for i in range(count):
            m = first + i
            own = kt[0] * own_w[pl.ds(m, 1), :].astype(jnp.bfloat16)
            sib = kt[1] * sib_w[pl.ds(m, 1), :].astype(jnp.bfloat16)
            total = jnp.dot(own, v_buf[0, c], preferred_element_type=jnp.float32)
            total += jnp.dot(sib, v_buf[1, c], preferred_element_type=jnp.float32)
            st[c, mem_rows(m, 1), :] = total

    def mem_rows(m, count):
        return pl.ds(pl.multiple_of(m * HDIM, HDIM), count * HDIM)

    landing = {"y": ybuf, "s": zbuf, "m": mbuf}

    def reduce_copy(k, way, m, count):
        c = chunks[k][0]
        slot = TAGS.index("r") * len(WAYS) + WAYS.index(way)
        return pltpu.make_async_remote_copy(
            sbuf.at[c, mem_rows(m, count)], landing[way].at[c, mem_rows(m, count)],
            p_send.at[k, slot], p_recv.at[k, slot], device_id=device(way), device_id_type=MESH,
        )

    def gather_copy(k, way, tag, m, count):
        c = chunks[k][0]
        slot = TAGS.index(tag) * len(WAYS) + WAYS.index(way)
        here = sh[c].at[pl.ds(m, count)]
        return pltpu.make_async_remote_copy(
            here, here, p_send.at[k, slot], p_recv.at[k, slot],
            device_id=device(way), device_id_type=MESH,
        )

    def run(order, end):
        sent = []
        outs = []
        fetched.clear()

        def give(k, way, m, count):
            c = chunks[k][0]
            copy = reduce_copy(k, way, m, count)
            copy.start()
            sent.append(copy)

        def pack(k, m, count):
            c = chunks[k][0]
            here = mem_rows(m, count)
            sbuf[c, here, :] = st[c, here, :].astype(jnp.bfloat16)

        def total(k, ways, m, count):
            c = chunks[k][0]
            here = mem_rows(m, count)
            value = st[c, here, :]
            for way in ways:
                value = value + landing[way][c, here, :].astype(jnp.float32)
            return value

        def forward(k, ways, m, count, ways_sum):
            c = chunks[k][0]
            sbuf[c, mem_rows(m, count), :] = total(k, ways_sum, m, count).astype(jnp.bfloat16)
            give(k, ways, m, count)

        def finish(k, ways_sum, m, count):
            c = chunks[k][0]
            value = total(k, ways_sum, m, count).astype(jnp.bfloat16)
            sh[c][pl.ds(m, count)] = value.reshape(count, HDIM, HDIM)

        def share(k, way, tag, m, count):
            copy = gather_copy(k, way, tag, m, count)
            copy.start()
            sent.append(copy)

        def got(k, way, m, count):
            reduce_copy(k, way, m, count).wait_recv()

        def have(k, way, tag, m, count):
            gather_copy(k, way, tag, m, count).wait_recv()

        def readout(slot):
            q_loads[slot].wait()
            head = own_head(slot)
            scale = gain_buf[pl.ds(head, 1), :]
            for b in range(blocks):
                here = pl.ds(b * BLOCK, BLOCK)
                pair = jnp.concatenate([sh[slot][ids[r, b]] for r in range(2)], axis=1)
                product = jnp.dot(q_buf[slot, here, :], pair, preferred_element_type=jnp.float32)
                gates = [levels[r, b].astype(jnp.float32) / GATE_DEN for r in range(2)]
                value = gates[0] * product[:, :HDIM] + gates[1] * product[:, HDIM:]
                square = jnp.mean(value * value, axis=-1, keepdims=True)
                result = value * lax.rsqrt(square + 1e-05) * scale
                o_buf[slot, here, :] = result.astype(jnp.bfloat16)
            copy = pltpu.make_async_copy(o_buf.at[slot], o_hbm.at[:, cols(head)], o_sem.at[slot])
            copy.start()
            outs.append(copy)

        def cross(c):
            return pltpu.make_async_remote_copy(
                sh[c], sh[HALF + c], c_send.at[c], c_recv.at[c],
                device_id=(group, sibling), device_id_type=MESH,
            )

        def stage(k, s):
            c, base, u, kind = chunks[k]
            if s == 10:
                cross(c).start()
                readout(c)
                return
            if s == 11:
                cross(c).wait_recv()
                readout(HALF + c)
                return
            if kind[0] == "Y":
                mine, away = base + y * 2 * u, base + (1 - y) * 2 * u
                near, far = mine + high * u, mine + (1 - high) * u
                near2, far2 = away + high * u, away + (1 - high) * u
                if s == 0:
                    fetch(c)
                    local(c, away, 2 * u)
                    pack(k, away, 2 * u)
                    give(k, "y", away, 2 * u)
                    local(c, mine, 2 * u)
                elif s == 1:
                    got(k, "y", mine, 2 * u)
                    here = mem_rows(mine, 2 * u)
                    if end and kind == "YM":
                        forward(k, "s", mine, 2 * u, ("y",))
                    elif end:
                        forward(k, "s", far, u, ("y",))
                elif s == 2:
                    got(k, "s", mine if kind == "YM" else far, 2 * u if kind == "YM" else u)
                    forward(k, "m", far, u, ("y", "s"))
                elif s == 3:
                    got(k, "m", near, u)
                    if kind == "YE":
                        forward(k, "s", near, u, ("y", "m"))
                    else:
                        finish(k, ("y", "s", "m"), near, u)
                        share(k, "m", "n", near, u)
                        share(k, "s", "n", near, u)
                        share(k, "y", "n", near, u)
                elif s == 4:
                    got(k, "s", near, u)
                    finish(k, ("y", "s"), near, u)
                    share(k, "s", "n", near, u)
                    share(k, "y", "n", near, u)
                elif s == 5:
                    if kind == "YE":
                        have(k, "s", "n", near, u)
                        share(k, "m", "n", near, u)
                        share(k, "y", "n", near, u)
                    else:
                        have(k, "m", "n", far, u)
                        share(k, "s", "f", far, u)
                        share(k, "y", "f", far, u)
                elif s == 6:
                    if end:
                        have(k, "s", "n", near, u)
                        share(k, "y", "n", near, u)
                    else:
                        have(k, "m", "n", far, u)
                        share(k, "s", "f", far, u)
                        share(k, "y", "f", far, u)
                elif s == 7:
                    have(k, "s", "f", far, u)
                    share(k, "y", "f", far, u)
                elif s == 8:
                    have(k, "y", "n", near2, u)
                    have(k, "y", "f", far2, u)
            else:
                near, far = base + high * 2 * u, base + (1 - high) * 2 * u
                mine, away = near + y * u, near + (1 - y) * u
                mine2, away2 = far + y * u, far + (1 - y) * u
                if s == 0:
                    fetch(c)
                    local(c, far, 2 * u)
                    if end and kind == "ZE":
                        pack(k, far, 2 * u)
                        give(k, "s", far, 2 * u)
                    local(c, near, 2 * u)
                    if end and kind == "ZM":
                        pack(k, base, 4 * u)
                        give(k, "s", base, 4 * u)
                elif kind == "ZE":
                    if s == 1:
                        got(k, "s", far, 2 * u)
                        forward(k, "m", far, 2 * u, ("s",))
                    elif s == 2:
                        got(k, "m", near, 2 * u)
                        forward(k, "s", near, 2 * u, ("m",))
                    elif s == 3 and end:
                        got(k, "s", near, 2 * u)
                        forward(k, "y", away, u, ("s",))
                    elif s == 4 and end:
                        got(k, "y", mine, u)
                        finish(k, ("s", "y"), mine, u)
                        share(k, "y", "n", mine, u)
                        share(k, "s", "n", mine, u)
                    elif s == 5 and end:
                        have(k, "y", "n", away, u)
                        share(k, "s", "f", away, u)
                    elif s == 4:
                        have(k, "s", "n", mine, u)
                        share(k, "m", "n", mine, u)
                    elif s == 5:
                        have(k, "s", "f", away, u)
                        share(k, "m", "f", away, u)
                    elif s == 6:
                        have(k, "m", "n", mine2, u)
                        share(k, "s", "h", mine2, u)
                    elif s == 7 and not end:
                        have(k, "m", "f", away2, u)
                        share(k, "s", "i", away2, u)
                    elif s == 7:
                        have(k, "s", "h", mine2, u)
                    elif s == 8 and end:
                        have(k, "s", "i", away2, u)
                else:
                    if s == 1:
                        got(k, "s", base, 4 * u)
                        forward(k, "m", far, 2 * u, ("s",))
                    elif s == 2:
                        got(k, "m", near, 2 * u)
                        forward(k, "y", away, u, ("s", "m"))
                    elif s == 3:
                        got(k, "y", mine, u)
                        finish(k, ("s", "m", "y"), mine, u)
                        share(k, "y", "n", mine, u)
                        share(k, "m", "n", mine, u)
                        share(k, "s", "n", mine, u)
                    elif s == 4:
                        have(k, "y", "n", away, u)
                        share(k, "m", "f", away, u)
                        share(k, "s", "f", away, u)
                    elif s == 5:
                        have(k, "m", "n", mine2, u)
                        share(k, "s", "h", mine2, u)
                    elif s == 6 and not end:
                        have(k, "m", "f", away2, u)
                        share(k, "s", "i", away2, u)
                    elif s == 6:
                        have(k, "s", "n", mine, u)
                    elif s == 7 and end:
                        have(k, "s", "f", away, u)
                    elif s == 8 and end:
                        have(k, "s", "h", mine2, u)
                        have(k, "s", "i", away2, u)

        for k, s in order:
            stage(k, s)
        for copy in sent:
            copy.wait_send()
        for c in range(HALF):
            cross(c).wait_send()
        for copy in outs:
            copy.wait()

    @pl.when(inner == 0)
    def _():
        run(order_end, True)

    @pl.when(inner == 1)
    def _():
        run(order_inner, False)

    xw.wait_send()
    for i in range(HALF):
        swaps[i][0].wait_send()
        swaps[i][1].wait_send()


def body(n, queries, keys, values, memory_ids, gate_levels, norm_gain):
    tok = queries.shape[0]
    masks = []
    mask = 2
    while mask < n:
        masks.append(mask)
        mask *= 2
    plain = tuple(masks)
    turned = (masks[1], masks[0]) + tuple(masks[2:])
    orders = [turned if c % 4 == 2 else plain for c in range(HALF)]
    steps = len(masks)
    bf = jnp.bfloat16
    dma = pltpu.SemaphoreType.DMA
    hbm = pl.BlockSpec(memory_space=pl.ANY)
    smem = pl.BlockSpec(memory_space=pltpu.SMEM)
    return pl.pallas_call(
        functools.partial(kernel, n, tok, orders),
        out_shape=jax.ShapeDtypeStruct((tok, HEADS * HDIM), bf),
        in_specs=[hbm, hbm, hbm, smem, smem, hbm],
        out_specs=hbm,
        scratch_shapes=[
            pltpu.VMEM((HEADS, tok, HDIM), bf),
            pltpu.VMEM((2, HALF, tok, HDIM), bf),
            pltpu.VMEM((2, HALF, tok, HDIM), bf),
            pltpu.VMEM((HEADS, tok, HDIM), bf),
            pltpu.VMEM((MEMS, tok), jnp.float32),
            pltpu.VMEM((MEMS, tok), jnp.float32),
            pltpu.VMEM((2, HDIM, tok), bf),
            pltpu.VMEM((HALF, ROWS, HDIM), jnp.float32),
            pltpu.VMEM((HALF, ROWS, HDIM), bf),
            pltpu.VMEM((HALF, ROWS, HDIM), bf),
            *[pltpu.VMEM((MEMS, HDIM, HDIM), bf) for _ in range(HEADS)],
            pltpu.VMEM((HEADS, HDIM), jnp.float32),
            dma((HEADS,)), dma((HALF,)), dma((HALF,)), dma((HEADS,)), dma((1,)),
            dma((HALF,)), dma((HALF,)), dma((HALF,)), dma((HALF,)), dma((1,)), dma((1,)),
            dma((HALF,)), dma((HALF,)),
            dma((HALF, steps)), dma((HALF, steps)), dma((HALF, steps)), dma((HALF, steps)),
        ],
        compiler_params=pltpu.CompilerParams(
            collective_id=0, has_side_effects=True, vmem_limit_bytes=48 * 1024 * 1024
        ),
        name="memory_readout",
    )(queries, keys, values, memory_ids.T, gate_levels.T, norm_gain.reshape(HEADS, HDIM))


def planned_body(queries, keys, values, memory_ids, gate_levels, norm_gain):
    tok = queries.shape[0]
    bf = jnp.bfloat16
    dma = pltpu.SemaphoreType.DMA
    hbm = pl.BlockSpec(memory_space=pl.ANY)
    smem = pl.BlockSpec(memory_space=pltpu.SMEM)
    kinds = len(TAGS) * len(WAYS)
    return pl.pallas_call(
        functools.partial(plan_kernel, tok, CHUNKS, ORDER_END, ORDER_INNER),
        out_shape=jax.ShapeDtypeStruct((tok, HEADS * HDIM), bf),
        in_specs=[hbm, hbm, hbm, smem, smem, hbm],
        out_specs=hbm,
        scratch_shapes=[
            pltpu.VMEM((HEADS, tok, HDIM), bf),
            pltpu.VMEM((2, HALF, tok, HDIM), bf),
            pltpu.VMEM((2, HALF, tok, HDIM), bf),
            pltpu.VMEM((HEADS, tok, HDIM), bf),
            pltpu.VMEM((MEMS, tok), jnp.float32),
            pltpu.VMEM((MEMS, tok), jnp.float32),
            pltpu.VMEM((2, HDIM, tok), bf),
            pltpu.VMEM((HALF, ROWS, HDIM), jnp.float32),
            *[pltpu.VMEM((HALF, ROWS, HDIM), bf) for _ in range(4)],
            *[pltpu.VMEM((MEMS, HDIM, HDIM), bf) for _ in range(HEADS)],
            pltpu.VMEM((HEADS, HDIM), jnp.float32),
            dma((HEADS,)), dma((HALF,)), dma((HALF,)), dma((HEADS,)), dma((1,)),
            dma((HALF,)), dma((HALF,)), dma((HALF,)), dma((HALF,)), dma((1,)), dma((1,)),
            dma((HALF,)), dma((HALF,)),
            dma((len(CHUNKS), kinds)), dma((len(CHUNKS), kinds)),
        ],
        compiler_params=pltpu.CompilerParams(
            collective_id=0, has_side_effects=True, vmem_limit_bytes=48 * 1024 * 1024
        ),
        name="memory_readout",
    )(queries, keys, values, memory_ids.T, gate_levels.T, norm_gain.reshape(HEADS, HDIM))


def solution(mesh):
    rows = P(("groups", "seq"), None)
    n = mesh.shape["seq"]
    part = planned_body if n == PLANNED else functools.partial(body, n)
    return jax.shard_map(
        part,
        mesh=mesh,
        in_specs=(rows, rows, rows, rows, rows, P()),
        out_specs=rows,
        check_vma=False,
    )
```

```python
import functools

import jax
import jax.numpy as jnp
from jax import lax
from jax.experimental import pallas as pl
from jax.experimental.pallas import tpu as pltpu
from jax.sharding import PartitionSpec as P

HEADS = 16
HDIM = 128
MEMS = 8
BLOCK = 64
GATE_DEN = 16
HALF = HEADS // 2
ROWS = MEMS * HDIM
GROUP = 12
LAG = 3
MESH = pl.DeviceIdType.MESH
TAGS = "rnfhi"
WAYS = "ysm"
PLANNED = 16
AHEAD = 3
CHUNKS = (
    (0, 0, 2, "ZE"),
    (1, 0, 2, "ZE"),
    (2, 0, 2, "YM"),
    (3, 0, 2, "YM"),
    (4, 0, 2, "YM"),
    (5, 0, 2, "YM"),
    (6, 0, 2, "YM"),
    (7, 0, 2, "YM"),
)
ORDER_END = (
    (0, 0), (2, 0), (1, 0), (3, 0), (4, 0), (2, 1), (5, 0), (3, 1), (6, 0), (4, 1), (7, 0), (5, 1),
    (0, 3), (6, 1), (2, 6), (7, 1), (1, 3), (0, 4), (2, 7), (1, 4), (3, 6), (0, 5), (1, 5), (4, 6),
    (2, 8), (5, 6), (4, 7), (2, 10), (3, 7), (2, 11), (6, 6), (4, 8), (5, 7), (3, 8), (3, 10), (6,
    7), (1, 7), (4, 10), (7, 6), (3, 11), (0, 7), (0, 8), (0, 10), (7, 7), (4, 11), (5, 8), (5, 10),
    (0, 11), (6, 8), (1, 8), (6, 10), (1, 10), (7, 8), (7, 10), (6, 11), (1, 11), (5, 11), (7, 11),
)
ORDER_INNER = (
    (2, 0), (0, 0), (3, 0), (1, 0), (0, 1), (4, 0), (2, 1), (5, 0), (1, 1), (0, 2), (3, 1), (2, 2),
    (6, 0), (4, 1), (7, 0), (1, 2), (3, 2), (2, 3), (4, 2), (3, 3), (5, 1), (5, 2), (6, 1), (4, 3),
    (2, 5), (3, 5), (7, 1), (6, 2), (5, 3), (4, 5), (6, 3), (2, 8), (2, 10), (7, 2), (0, 4), (3, 8),
    (1, 4), (3, 10), (5, 5), (4, 8), (6, 5), (2, 11), (4, 10), (0, 5), (7, 3), (3, 11), (0, 6), (5,
    8), (4, 11), (1, 5), (1, 6), (5, 10), (5, 11), (0, 7), (7, 5), (1, 7), (7, 8), (6, 8), (6, 10),
    (0, 8), (1, 8), (7, 10), (0, 10), (1, 10), (1, 11), (7, 11), (6, 11), (0, 11),
)


def kernel(
    n, tok, orders,
    q_hbm, k_hbm, v_hbm, ids, levels, gain,
    o_hbm,
    q_buf, k_buf, v_buf, o_buf, own_w, sib_w, kt, st, sbuf, rbuf,
    sh0, sh1, sh2, sh3, sh4, sh5, sh6, sh7, sh8, sh9, sh10, sh11, sh12, sh13, sh14, sh15,
    gain_buf, q_sem, k_sem, v_sem, o_sem, n_sem,
    xk_send, xk_recv, xv_send, xv_recv, xw_send, xw_recv,
    c_send, c_recv, r_send, r_recv, g_send, g_recv,
):
    sh = (sh0, sh1, sh2, sh3, sh4, sh5, sh6, sh7, sh8, sh9, sh10, sh11, sh12, sh13, sh14, sh15)
    group = lax.axis_index("groups")
    me = lax.axis_index("seq")
    core = me % 2
    sibling = me + 1 - 2 * core
    steps = len(orders[0])

    def bit(mask):
        return (me // mask) % 2

    def partner(mask):
        return (group, me + mask - 2 * mask * bit(mask))

    def cols(head):
        return pl.ds(pl.multiple_of(head * HDIM, HDIM), HDIM)

    def own_head(slot):
        return core * HALF + slot if slot < HALF else (1 - core) * HALF + slot - HALF

    loads = []
    for i in range(HALF):
        kc = pltpu.make_async_copy(k_hbm.at[:, cols(own_head(i))], k_buf.at[0, i], k_sem.at[i])
        vc = pltpu.make_async_copy(v_hbm.at[:, cols(own_head(i))], v_buf.at[0, i], v_sem.at[i])
        kc.start()
        vc.start()
        loads.append((kc, vc))

    gain_load = pltpu.make_async_copy(gain, gain_buf, n_sem.at[0])
    gain_load.start()

    barrier = pltpu.get_barrier_semaphore()
    masks = [1] + sorted(orders[0])
    for mask in masks:
        pl.semaphore_signal(barrier, inc=1, device_id=partner(mask), device_id_type=MESH)

    blocks = tok // BLOCK
    member = lax.broadcasted_iota(jnp.int32, (MEMS, 2 * BLOCK), 0)
    lane = lax.broadcasted_iota(jnp.int32, (MEMS, 2 * BLOCK), 1)
    for p in range(blocks // 2):
        w = []
        for b in (2 * p, 2 * p + 1):
            w.append(
                jnp.where(member == ids[0, b], levels[0, b], 0)
                + jnp.where(member == ids[1, b], levels[1, b], 0)
            )
        both = jnp.where(lane < BLOCK, w[0], w[1]).astype(jnp.float32) / GATE_DEN
        own_w[:, p * 2 * BLOCK : (p + 1) * 2 * BLOCK] = both

    gain_load.wait()
    pl.semaphore_wait(barrier, len(masks))

    xw = pltpu.make_async_remote_copy(
        own_w, sib_w, xw_send.at[0], xw_recv.at[0], device_id=(group, sibling), device_id_type=MESH
    )
    xw.start()
    swaps = []
    for i in range(HALF):
        other = (1 - core) * HALF + i
        kc = pltpu.make_async_remote_copy(
            k_hbm.at[:, cols(other)], k_buf.at[1, i], xk_send.at[i], xk_recv.at[i],
            device_id=(group, sibling), device_id_type=MESH,
        )
        vc = pltpu.make_async_remote_copy(
            v_hbm.at[:, cols(other)], v_buf.at[1, i], xv_send.at[i], xv_recv.at[i],
            device_id=(group, sibling), device_id_type=MESH,
        )
        kc.start()
        vc.start()
        swaps.append((kc, vc))
    q_loads = []
    for slot in range(HEADS):
        qc = pltpu.make_async_copy(q_hbm.at[:, cols(own_head(slot))], q_buf.at[slot], q_sem.at[slot])
        qc.start()
        q_loads.append(qc)

    def local_state(c):
        for copy in loads[c]:
            copy.wait()
        if c == 0:
            xw.wait_recv()
        for copy in swaps[c]:
            copy.wait_recv()
        kt[0] = k_buf[0, c].T
        kt[1] = k_buf[1, c].T

        def one(m, carry):
            own = kt[0] * own_w[pl.ds(m, 1), :].astype(jnp.bfloat16)
            sib = kt[1] * sib_w[pl.ds(m, 1), :].astype(jnp.bfloat16)
            total = jnp.dot(own, v_buf[0, c], preferred_element_type=jnp.float32)
            total += jnp.dot(sib, v_buf[1, c], preferred_element_type=jnp.float32)
            st[c, pl.ds(pl.multiple_of(m * HDIM, HDIM), HDIM), :] = total
            return carry

        lax.fori_loop(0, MEMS, one, 0, unroll=4)

    low = [0] * HALF
    lows = [[] for _ in range(HALF)]
    reduces = [[] for _ in range(HALF)]
    gathers = [dict() for _ in range(HALF)]

    def rows(start, size):
        return pl.ds(pl.multiple_of(start, size), size)

    def part(start, size):
        if size >= HDIM:
            return (pl.ds(start // HDIM, size // HDIM),)
        return (start // HDIM, rows(start % HDIM, size))

    def send_half(c, s):
        size = ROWS >> (s + 1)
        b = bit(orders[c][s])
        lows[c].append(low[c])
        away = rows(low[c] + (1 - b) * size, size)
        low[c] = low[c] + b * size
        sbuf[c, away, :] = st[c, away, :].astype(jnp.bfloat16)
        copy = pltpu.make_async_remote_copy(
            sbuf.at[c, away], rbuf.at[c, size : 2 * size],
            r_send.at[c, s], r_recv.at[c, s],
            device_id=partner(orders[c][s]), device_id_type=MESH,
        )
        copy.start()
        reduces[c].append(copy)

    def gather(c, s):
        size = ROWS >> (s + 1)
        b = bit(orders[c][s])
        have = part(lows[c][s] + b * size, size)
        copy = pltpu.make_async_remote_copy(
            sh[c].at[*have], sh[c].at[*have],
            g_send.at[c, s], g_recv.at[c, s],
            device_id=partner(orders[c][s]), device_id_type=MESH,
        )
        copy.start()
        gathers[c][s] = copy

    cores = {}
    outs = []

    def readout(slot):
        q_loads[slot].wait()
        head = own_head(slot)
        scale = gain_buf[pl.ds(head, 1), :]

        def one(g, carry):
            for b in range(GROUP):
                b = g * GROUP + b
                here = pl.ds(pl.multiple_of(b * BLOCK, BLOCK), BLOCK)
                pair = jnp.concatenate(
                    [
                        sh[slot][ids[r, b]]
                        for r in range(2)
                    ],
                    axis=1,
                )
                product = jnp.dot(q_buf[slot, here, :], pair, preferred_element_type=jnp.float32)
                gates = [levels[r, b].astype(jnp.float32) / GATE_DEN for r in range(2)]
                total = gates[0] * product[:, :HDIM] + gates[1] * product[:, HDIM:]
                square = jnp.mean(total * total, axis=-1, keepdims=True)
                result = total * lax.rsqrt(square + 1e-05) * scale
                o_buf[slot, here, :] = result.astype(jnp.bfloat16)
            return carry

        lax.fori_loop(0, blocks // GROUP, one, 0)
        copy = pltpu.make_async_copy(o_buf.at[slot], o_hbm.at[:, cols(head)], o_sem.at[slot])
        copy.start()
        outs.append(copy)

    def stage(c, k):
        if k == 0:
            local_state(c)
            send_half(c, 0)
        elif k <= steps:
            s = k - 1
            size = ROWS >> (s + 1)
            reduces[c][s].wait_recv()
            keep = rows(low[c], size)
            total = st[c, keep, :] + rbuf[c, size : 2 * size, :].astype(jnp.float32)
            if k < steps:
                st[c, keep, :] = total
                send_half(c, k)
            else:
                owned = total.astype(jnp.bfloat16)
                if size >= HDIM:
                    owned = owned.reshape(size // HDIM, HDIM, HDIM)
                sh[c][part(low[c], size)] = owned
                gather(c, steps - 1)
        elif k < 2 * steps:
            s = 2 * steps - k
            gathers[c][s].wait_recv()
            gather(c, s - 1)
        elif k == 2 * steps:
            gathers[c][0].wait_recv()
            copy = pltpu.make_async_remote_copy(
                sh[c], sh[HALF + c], c_send.at[c], c_recv.at[c],
                device_id=(group, sibling), device_id_type=MESH,
            )
            copy.start()
            cores[c] = copy
            readout(c)
        else:
            cores[c].wait_recv()
            readout(HALF + c)

    plan = [(c + LAG * k, -k, c) for c in range(HALF) for k in range(2 * steps + 2)]
    for _, k, c in sorted(plan):
        stage(c, -k)

    xw.wait_send()
    for i in range(HALF):
        swaps[i][0].wait_send()
        swaps[i][1].wait_send()
        cores[i].wait_send()
        for s in range(steps):
            reduces[i][s].wait_send()
            gathers[i][s].wait_send()
    for copy in outs:
        copy.wait()


def plan_kernel(
    tok, chunks, order_end, order_inner,
    q_hbm, k_hbm, v_hbm, ids_hbm, levels_hbm, gain,
    out,
    ids, levels, sib_ids, sib_levels, q_buf, k_buf, v_buf, own_w, sib_w, kt, st, sbuf, ybuf, zbuf, mbuf,
    sh0, sh1, sh2, sh3, sh4, sh5, sh6, sh7, sh8, sh9, sh10, sh11, sh12, sh13, sh14, sh15,
    gain_buf, q_sem, k_sem, v_sem, n_sem,
    xk_send, xk_recv, xv_send, xv_recv, xw_send, xw_recv,
    c_send, c_recv, p_send, p_recv,
):
    sh = (sh0, sh1, sh2, sh3, sh4, sh5, sh6, sh7, sh8, sh9, sh10, sh11, sh12, sh13, sh14, sh15)
    group = lax.axis_index("groups")
    me = lax.axis_index("seq")
    core = me % 2
    y = (me // 2) % 2
    z = me // 4
    high = z // 2
    inner = (z + high) % 2
    sibling = me + 1 - 2 * core
    towards = {
        "y": me + 2 - 4 * y,
        "s": me + 4 - 8 * (z % 2),
        "m": me + 4 * (3 - 2 * z),
    }

    def device(way):
        return (group, towards[way])

    def cols(head):
        return pl.ds(pl.multiple_of(head * HDIM, HDIM), HDIM)

    def own_head(slot):
        return core * HALF + slot if slot < HALF else (1 - core) * HALF + slot - HALF

    barrier = pltpu.get_barrier_semaphore()
    pl.semaphore_signal(barrier, inc=1, device_id=(group, sibling), device_id_type=MESH)
    pl.semaphore_signal(barrier, inc=1, device_id=device("y"), device_id_type=MESH)
    pl.semaphore_signal(barrier, inc=1, device_id=device("s"), device_id_type=MESH)

    @pl.when(inner == 1)
    def _():
        pl.semaphore_signal(barrier, inc=1, device_id=device("m"), device_id_type=MESH)

    loads = []
    swaps = []
    q_loads = []
    for i in range(HALF):
        mine, other = cols(own_head(i)), cols((1 - core) * HALF + i)
        pairs = ((k_hbm, k_buf, k_sem, xk_send, xk_recv), (v_hbm, v_buf, v_sem, xv_send, xv_recv))
        loads.append([
            pltpu.make_async_copy(hbm.at[:, mine], buf.at[0, i], sem.at[i])
            for hbm, buf, sem, _, _ in pairs
        ])
        swaps.append([
            pltpu.make_async_remote_copy(
                hbm.at[:, other], buf.at[1, i], send.at[i], recv.at[i],
                device_id=(group, sibling), device_id_type=MESH,
            )
            for hbm, buf, _, send, recv in pairs
        ])
    for slot in range(HEADS):
        q_loads.append(
            pltpu.make_async_copy(q_hbm.at[:, cols(own_head(slot))], q_buf.at[slot], q_sem.at[slot])
        )

    def start(copies):
        for copy in copies:
            copy.start()

    small = [
        pltpu.make_async_copy(ids_hbm, ids, n_sem.at[0]),
        pltpu.make_async_copy(levels_hbm, levels, n_sem.at[1]),
        pltpu.make_async_copy(gain, gain_buf, n_sem.at[2]),
    ]

    start(small)
    start(loads[0])
    pl.semaphore_wait(barrier, 3 + inner)
    lists = [
        pltpu.make_async_remote_copy(
            hbm, there, xw_send.at[i], xw_recv.at[i],
            device_id=(group, sibling), device_id_type=MESH,
        )
        for i, (hbm, there) in enumerate(((ids_hbm, sib_ids), (levels_hbm, sib_levels)))
    ]
    start(lists)
    start(swaps[0])
    for i in range(1, AHEAD):
        start(loads[i])
        start(swaps[i])

    blocks = tok // BLOCK
    member = lax.broadcasted_iota(jnp.int32, (MEMS, 2 * BLOCK), 0)
    lane = lax.broadcasted_iota(jnp.int32, (MEMS, 2 * BLOCK), 1)

    def weigh(to, names, amounts):
        for p in range(blocks // 2):
            w = []
            for b in (2 * p, 2 * p + 1):
                w.append(
                    jnp.where(member == names[0, b], amounts[0, b], 0)
                    + jnp.where(member == names[1, b], amounts[1, b], 0)
                )
            both = jnp.where(lane < BLOCK, w[0], w[1]).astype(jnp.float32) / GATE_DEN
            to[:, p * 2 * BLOCK : (p + 1) * 2 * BLOCK] = both

    for copy in small:
        copy.wait()
    weigh(own_w, ids, levels)
    for copy in lists:
        copy.wait_recv()
    weigh(sib_w, sib_ids, sib_levels)

    fetched = set()
    asked = set()

    def fetch(c):
        if c in fetched:
            return
        for copy in loads[c]:
            copy.wait()
        fetched.add(c)
        kt[0] = k_buf[0, c].T
        for copy in swaps[c]:
            copy.wait_recv()
        if c + AHEAD < HALF:
            start(loads[c + AHEAD])
            start(swaps[c + AHEAD])
        kt[1] = k_buf[1, c].T

    def ask(c):
        if c not in asked:
            asked.add(c)
            start([q_loads[c], q_loads[HALF + c]])

    def local(c, first, count):
        for i in range(count):
            m = first + i
            own = kt[0] * own_w[pl.ds(m, 1), :].astype(jnp.bfloat16)
            sib = kt[1] * sib_w[pl.ds(m, 1), :].astype(jnp.bfloat16)
            total = jnp.dot(own, v_buf[0, c], preferred_element_type=jnp.float32)
            total += jnp.dot(sib, v_buf[1, c], preferred_element_type=jnp.float32)
            st[c, mem_rows(m, 1), :] = total

    def mem_rows(m, count):
        return pl.ds(pl.multiple_of(m * HDIM, HDIM), count * HDIM)

    landing = {"y": ybuf, "s": zbuf, "m": mbuf}

    def reduce_copy(k, way, m, count):
        c = chunks[k][0]
        slot = TAGS.index("r") * len(WAYS) + WAYS.index(way)
        return pltpu.make_async_remote_copy(
            sbuf.at[c, mem_rows(m, count)], landing[way].at[c, mem_rows(m, count)],
            p_send.at[k, slot], p_recv.at[k, slot], device_id=device(way), device_id_type=MESH,
        )

    def gather_copy(k, way, tag, m, count):
        c = chunks[k][0]
        slot = TAGS.index(tag) * len(WAYS) + WAYS.index(way)
        here = sh[c].at[pl.ds(m, count)]
        return pltpu.make_async_remote_copy(
            here, here, p_send.at[k, slot], p_recv.at[k, slot],
            device_id=device(way), device_id_type=MESH,
        )

    def run(order, end):
        sent = []
        fetched.clear()
        asked.clear()

        def give(k, way, m, count):
            c = chunks[k][0]
            copy = reduce_copy(k, way, m, count)
            copy.start()
            sent.append(copy)

        def pack(k, m, count):
            c = chunks[k][0]
            here = mem_rows(m, count)
            sbuf[c, here, :] = st[c, here, :].astype(jnp.bfloat16)

        def total(k, ways, m, count):
            c = chunks[k][0]
            here = mem_rows(m, count)
            value = st[c, here, :]
            for way in ways:
                value = value + landing[way][c, here, :].astype(jnp.float32)
            return value

        def forward(k, ways, m, count, ways_sum):
            c = chunks[k][0]
            sbuf[c, mem_rows(m, count), :] = total(k, ways_sum, m, count).astype(jnp.bfloat16)
            give(k, ways, m, count)

        def finish(k, ways_sum, m, count):
            c = chunks[k][0]
            value = total(k, ways_sum, m, count).astype(jnp.bfloat16)
            sh[c][pl.ds(m, count)] = value.reshape(count, HDIM, HDIM)

        def share(k, way, tag, m, count):
            copy = gather_copy(k, way, tag, m, count)
            copy.start()
            sent.append(copy)

        def got(k, way, m, count):
            reduce_copy(k, way, m, count).wait_recv()

        def have(k, way, tag, m, count):
            gather_copy(k, way, tag, m, count).wait_recv()

        def readout(slot):
            q_loads[slot].wait()
            head = own_head(slot)
            scale = gain_buf[pl.ds(head, 1), :]
            for b in range(blocks):
                here = pl.ds(b * BLOCK, BLOCK)
                pair = jnp.concatenate([sh[slot][ids[r, b]] for r in range(2)], axis=1)
                product = jnp.dot(q_buf[slot, here, :], pair, preferred_element_type=jnp.float32)
                gates = [levels[r, b].astype(jnp.float32) / GATE_DEN for r in range(2)]
                value = gates[0] * product[:, :HDIM] + gates[1] * product[:, HDIM:]
                square = jnp.mean(value * value, axis=-1, keepdims=True)
                result = value * lax.rsqrt(square + 1e-05) * scale
                out[here, cols(head)] = result.astype(jnp.bfloat16)

        def cross(c):
            return pltpu.make_async_remote_copy(
                sh[c], sh[HALF + c], c_send.at[c], c_recv.at[c],
                device_id=(group, sibling), device_id_type=MESH,
            )

        def stage(k, s):
            c, base, u, kind = chunks[k]
            if s == 10:
                cross(c).start()
                readout(c)
                return
            if s == 11:
                cross(c).wait_recv()
                readout(HALF + c)
                return
            if kind[0] == "Y":
                mine, away = base + y * 2 * u, base + (1 - y) * 2 * u
                near, far = mine + high * u, mine + (1 - high) * u
                near2, far2 = away + high * u, away + (1 - high) * u
                if s == 0:
                    fetch(c)
                    local(c, away, 2 * u)
                    pack(k, away, 2 * u)
                    give(k, "y", away, 2 * u)
                    local(c, mine, 2 * u)
                    ask(c)
                elif s == 1:
                    got(k, "y", mine, 2 * u)
                    here = mem_rows(mine, 2 * u)
                    if end and kind == "YM":
                        forward(k, "s", mine, 2 * u, ("y",))
                    elif end:
                        forward(k, "s", far, u, ("y",))
                elif s == 2:
                    got(k, "s", mine if kind == "YM" else far, 2 * u if kind == "YM" else u)
                    forward(k, "m", far, u, ("y", "s"))
                elif s == 3:
                    got(k, "m", near, u)
                    if kind == "YE":
                        forward(k, "s", near, u, ("y", "m"))
                    else:
                        finish(k, ("y", "s", "m"), near, u)
                        share(k, "m", "n", near, u)
                        share(k, "s", "n", near, u)
                        share(k, "y", "n", near, u)
                elif s == 4:
                    got(k, "s", near, u)
                    finish(k, ("y", "s"), near, u)
                    share(k, "s", "n", near, u)
                    share(k, "y", "n", near, u)
                elif s == 5:
                    if kind == "YE":
                        have(k, "s", "n", near, u)
                        share(k, "m", "n", near, u)
                        share(k, "y", "n", near, u)
                    else:
                        have(k, "m", "n", far, u)
                        share(k, "s", "f", far, u)
                        share(k, "y", "f", far, u)
                elif s == 6:
                    if end:
                        have(k, "s", "n", near, u)
                        share(k, "y", "n", near, u)
                    else:
                        have(k, "m", "n", far, u)
                        share(k, "s", "f", far, u)
                        share(k, "y", "f", far, u)
                elif s == 7:
                    have(k, "s", "f", far, u)
                    share(k, "y", "f", far, u)
                elif s == 8:
                    have(k, "y", "n", near2, u)
                    have(k, "y", "f", far2, u)
            else:
                near, far = base + high * 2 * u, base + (1 - high) * 2 * u
                mine, away = near + y * u, near + (1 - y) * u
                mine2, away2 = far + y * u, far + (1 - y) * u
                if s == 0:
                    fetch(c)
                    local(c, far, 2 * u)
                    if end and kind == "ZE":
                        pack(k, far, 2 * u)
                        give(k, "s", far, 2 * u)
                    local(c, near, 2 * u)
                    if end and kind == "ZM":
                        pack(k, base, 4 * u)
                        give(k, "s", base, 4 * u)
                    ask(c)
                elif kind == "ZE":
                    if s == 1:
                        got(k, "s", far, 2 * u)
                        forward(k, "m", far, 2 * u, ("s",))
                    elif s == 2:
                        got(k, "m", near, 2 * u)
                        forward(k, "s", near, 2 * u, ("m",))
                    elif s == 3 and end:
                        got(k, "s", near, 2 * u)
                        forward(k, "y", away, u, ("s",))
                    elif s == 4 and end:
                        got(k, "y", mine, u)
                        finish(k, ("s", "y"), mine, u)
                        share(k, "y", "n", mine, u)
                        share(k, "s", "n", mine, u)
                    elif s == 5 and end:
                        have(k, "y", "n", away, u)
                        share(k, "s", "f", away, u)
                    elif s == 4:
                        have(k, "s", "n", mine, u)
                        share(k, "m", "n", mine, u)
                    elif s == 5:
                        have(k, "s", "f", away, u)
                        share(k, "m", "f", away, u)
                    elif s == 6:
                        have(k, "m", "n", mine2, u)
                        share(k, "s", "h", mine2, u)
                    elif s == 7 and not end:
                        have(k, "m", "f", away2, u)
                        share(k, "s", "i", away2, u)
                    elif s == 7:
                        have(k, "s", "h", mine2, u)
                    elif s == 8 and end:
                        have(k, "s", "i", away2, u)
                else:
                    if s == 1:
                        got(k, "s", base, 4 * u)
                        forward(k, "m", far, 2 * u, ("s",))
                    elif s == 2:
                        got(k, "m", near, 2 * u)
                        forward(k, "y", away, u, ("s", "m"))
                    elif s == 3:
                        got(k, "y", mine, u)
                        finish(k, ("s", "m", "y"), mine, u)
                        share(k, "y", "n", mine, u)
                        share(k, "m", "n", mine, u)
                        share(k, "s", "n", mine, u)
                    elif s == 4:
                        have(k, "y", "n", away, u)
                        share(k, "m", "f", away, u)
                        share(k, "s", "f", away, u)
                    elif s == 5:
                        have(k, "m", "n", mine2, u)
                        share(k, "s", "h", mine2, u)
                    elif s == 6 and not end:
                        have(k, "m", "f", away2, u)
                        share(k, "s", "i", away2, u)
                    elif s == 6:
                        have(k, "s", "n", mine, u)
                    elif s == 7 and end:
                        have(k, "s", "f", away, u)
                    elif s == 8 and end:
                        have(k, "s", "h", mine2, u)
                        have(k, "s", "i", away2, u)

        for k, s in order:
            stage(k, s)
        for copy in sent:
            copy.wait_send()
        for c in range(HALF):
            cross(c).wait_send()

    @pl.when(inner == 0)
    def _():
        run(order_end, True)

    @pl.when(inner == 1)
    def _():
        run(order_inner, False)

    for copy in lists:
        copy.wait_send()
    for i in range(HALF):
        swaps[i][0].wait_send()
        swaps[i][1].wait_send()


def body(n, queries, keys, values, memory_ids, gate_levels, norm_gain):
    tok = queries.shape[0]
    masks = []
    mask = 2
    while mask < n:
        masks.append(mask)
        mask *= 2
    plain = tuple(masks)
    turned = (masks[1], masks[0]) + tuple(masks[2:])
    orders = [turned if c % 4 == 2 else plain for c in range(HALF)]
    steps = len(masks)
    bf = jnp.bfloat16
    dma = pltpu.SemaphoreType.DMA
    hbm = pl.BlockSpec(memory_space=pl.ANY)
    smem = pl.BlockSpec(memory_space=pltpu.SMEM)
    return pl.pallas_call(
        functools.partial(kernel, n, tok, orders),
        out_shape=jax.ShapeDtypeStruct((tok, HEADS * HDIM), bf),
        in_specs=[hbm, hbm, hbm, smem, smem, hbm],
        out_specs=hbm,
        scratch_shapes=[
            pltpu.VMEM((HEADS, tok, HDIM), bf),
            pltpu.VMEM((2, HALF, tok, HDIM), bf),
            pltpu.VMEM((2, HALF, tok, HDIM), bf),
            pltpu.VMEM((HEADS, tok, HDIM), bf),
            pltpu.VMEM((MEMS, tok), jnp.float32),
            pltpu.VMEM((MEMS, tok), jnp.float32),
            pltpu.VMEM((2, HDIM, tok), bf),
            pltpu.VMEM((HALF, ROWS, HDIM), jnp.float32),
            pltpu.VMEM((HALF, ROWS, HDIM), bf),
            pltpu.VMEM((HALF, ROWS, HDIM), bf),
            *[pltpu.VMEM((MEMS, HDIM, HDIM), bf) for _ in range(HEADS)],
            pltpu.VMEM((HEADS, HDIM), jnp.float32),
            dma((HEADS,)), dma((HALF,)), dma((HALF,)), dma((HEADS,)), dma((1,)),
            dma((HALF,)), dma((HALF,)), dma((HALF,)), dma((HALF,)), dma((1,)), dma((1,)),
            dma((HALF,)), dma((HALF,)),
            dma((HALF, steps)), dma((HALF, steps)), dma((HALF, steps)), dma((HALF, steps)),
        ],
        compiler_params=pltpu.CompilerParams(
            collective_id=0, has_side_effects=True, vmem_limit_bytes=48 * 1024 * 1024
        ),
        name="memory_readout",
    )(queries, keys, values, memory_ids.T, gate_levels.T, norm_gain.reshape(HEADS, HDIM))


def planned_body(queries, keys, values, memory_ids, gate_levels, norm_gain):
    tok = queries.shape[0]
    bf = jnp.bfloat16
    dma = pltpu.SemaphoreType.DMA
    hbm = pl.BlockSpec(memory_space=pltpu.HBM)
    kinds = len(TAGS) * len(WAYS)
    return pl.pallas_call(
        functools.partial(plan_kernel, tok, CHUNKS, ORDER_END, ORDER_INNER),
        out_shape=jax.ShapeDtypeStruct((tok, HEADS * HDIM), bf),
        in_specs=[hbm] * 6,
        out_specs=pl.BlockSpec(memory_space=pltpu.VMEM),
        scratch_shapes=[
            *[pltpu.SMEM((2, tok // BLOCK), jnp.int32) for _ in range(4)],
            pltpu.VMEM((HEADS, tok, HDIM), bf),
            pltpu.VMEM((2, HALF, tok, HDIM), bf),
            pltpu.VMEM((2, HALF, tok, HDIM), bf),
            pltpu.VMEM((MEMS, tok), jnp.float32),
            pltpu.VMEM((MEMS, tok), jnp.float32),
            pltpu.VMEM((2, HDIM, tok), bf),
            pltpu.VMEM((HALF, ROWS, HDIM), jnp.float32),
            *[pltpu.VMEM((HALF, ROWS, HDIM), bf) for _ in range(4)],
            *[pltpu.VMEM((MEMS, HDIM, HDIM), bf) for _ in range(HEADS)],
            pltpu.VMEM((HEADS, HDIM), jnp.float32),
            dma((HEADS,)), dma((HALF,)), dma((HALF,)), dma((3,)),
            dma((HALF,)), dma((HALF,)), dma((HALF,)), dma((HALF,)), dma((2,)), dma((2,)),
            dma((HALF,)), dma((HALF,)),
            dma((len(CHUNKS), kinds)), dma((len(CHUNKS), kinds)),
        ],
        compiler_params=pltpu.CompilerParams(
            collective_id=0, has_side_effects=True, vmem_limit_bytes=48 * 1024 * 1024
        ),
        name="memory_readout",
    )(queries, keys, values, memory_ids.T, gate_levels.T, norm_gain.reshape(HEADS, HDIM))


def solution(mesh):
    rows = P(("groups", "seq"), None)
    n = mesh.shape["seq"]
    part = planned_body if n == PLANNED else functools.partial(body, n)
    return jax.shard_map(
        part,
        mesh=mesh,
        in_specs=(rows, rows, rows, rows, rows, P()),
        out_specs=rows,
        check_vma=False,
    )
```

```python
import functools

import jax
import jax.numpy as jnp
from jax import lax
from jax.experimental import pallas as pl
from jax.experimental.pallas import tpu as pltpu
from jax.sharding import PartitionSpec as P

HEADS = 16
HDIM = 128
MEMS = 8
BLOCK = 64
GATE_DEN = 16
HALF = HEADS // 2
ROWS = MEMS * HDIM
GROUP = 12
LAG = 3
MESH = pl.DeviceIdType.MESH
TAGS = "rnfhi"
WAYS = "ysm"
PLANNED = 16
AHEAD = 8
CHUNKS = (
    (0, 0, 2, "ZE"),
    (1, 0, 2, "ZE"),
    (2, 0, 2, "YM"),
    (3, 0, 2, "YM"),
    (4, 0, 2, "YM"),
    (5, 0, 2, "YM"),
    (6, 0, 2, "YM"),
    (7, 0, 2, "YM"),
)
ORDER_END = (
    (0, 0), (2, 0), (1, 0), (3, 0), (4, 0), (2, 1), (5, 0), (3, 1), (6, 0), (4, 1), (7, 0), (5, 1),
    (0, 3), (6, 1), (2, 6), (7, 1), (1, 3), (0, 4), (2, 7), (1, 4), (3, 6), (0, 5), (1, 5), (4, 6),
    (2, 8), (5, 6), (4, 7), (2, 10), (3, 7), (2, 11), (6, 6), (4, 8), (5, 7), (3, 8), (3, 10), (6,
    7), (1, 7), (4, 10), (7, 6), (3, 11), (0, 7), (0, 8), (0, 10), (7, 7), (4, 11), (5, 8), (5, 10),
    (0, 11), (6, 8), (1, 8), (6, 10), (1, 10), (7, 8), (7, 10), (6, 11), (1, 11), (5, 11), (7, 11),
)
ORDER_INNER = (
    (2, 0), (0, 0), (3, 0), (1, 0), (0, 1), (4, 0), (2, 1), (5, 0), (1, 1), (0, 2), (3, 1), (2, 2),
    (6, 0), (4, 1), (7, 0), (1, 2), (3, 2), (2, 3), (4, 2), (3, 3), (5, 1), (5, 2), (6, 1), (4, 3),
    (2, 5), (3, 5), (7, 1), (6, 2), (5, 3), (4, 5), (6, 3), (2, 8), (2, 10), (7, 2), (0, 4), (3, 8),
    (1, 4), (3, 10), (5, 5), (4, 8), (6, 5), (2, 11), (4, 10), (0, 5), (7, 3), (3, 11), (0, 6), (5,
    8), (4, 11), (1, 5), (1, 6), (5, 10), (5, 11), (0, 7), (7, 5), (1, 7), (7, 8), (6, 8), (6, 10),
    (0, 8), (1, 8), (7, 10), (0, 10), (1, 10), (1, 11), (7, 11), (6, 11), (0, 11),
)


def kernel(
    n, tok, orders,
    q_hbm, k_hbm, v_hbm, ids, levels, gain,
    o_hbm,
    q_buf, k_buf, v_buf, o_buf, own_w, sib_w, kt, st, sbuf, rbuf,
    sh0, sh1, sh2, sh3, sh4, sh5, sh6, sh7, sh8, sh9, sh10, sh11, sh12, sh13, sh14, sh15,
    gain_buf, q_sem, k_sem, v_sem, o_sem, n_sem,
    xk_send, xk_recv, xv_send, xv_recv, xw_send, xw_recv,
    c_send, c_recv, r_send, r_recv, g_send, g_recv,
):
    sh = (sh0, sh1, sh2, sh3, sh4, sh5, sh6, sh7, sh8, sh9, sh10, sh11, sh12, sh13, sh14, sh15)
    group = lax.axis_index("groups")
    me = lax.axis_index("seq")
    core = me % 2
    sibling = me + 1 - 2 * core
    steps = len(orders[0])

    def bit(mask):
        return (me // mask) % 2

    def partner(mask):
        return (group, me + mask - 2 * mask * bit(mask))

    def cols(head):
        return pl.ds(pl.multiple_of(head * HDIM, HDIM), HDIM)

    def own_head(slot):
        return core * HALF + slot if slot < HALF else (1 - core) * HALF + slot - HALF

    loads = []
    for i in range(HALF):
        kc = pltpu.make_async_copy(k_hbm.at[:, cols(own_head(i))], k_buf.at[0, i], k_sem.at[i])
        vc = pltpu.make_async_copy(v_hbm.at[:, cols(own_head(i))], v_buf.at[0, i], v_sem.at[i])
        kc.start()
        vc.start()
        loads.append((kc, vc))

    gain_load = pltpu.make_async_copy(gain, gain_buf, n_sem.at[0])
    gain_load.start()

    barrier = pltpu.get_barrier_semaphore()
    masks = [1] + sorted(orders[0])
    for mask in masks:
        pl.semaphore_signal(barrier, inc=1, device_id=partner(mask), device_id_type=MESH)

    blocks = tok // BLOCK
    member = lax.broadcasted_iota(jnp.int32, (MEMS, 2 * BLOCK), 0)
    lane = lax.broadcasted_iota(jnp.int32, (MEMS, 2 * BLOCK), 1)
    for p in range(blocks // 2):
        w = []
        for b in (2 * p, 2 * p + 1):
            w.append(
                jnp.where(member == ids[0, b], levels[0, b], 0)
                + jnp.where(member == ids[1, b], levels[1, b], 0)
            )
        both = jnp.where(lane < BLOCK, w[0], w[1]).astype(jnp.float32) / GATE_DEN
        own_w[:, p * 2 * BLOCK : (p + 1) * 2 * BLOCK] = both

    gain_load.wait()
    pl.semaphore_wait(barrier, len(masks))

    xw = pltpu.make_async_remote_copy(
        own_w, sib_w, xw_send.at[0], xw_recv.at[0], device_id=(group, sibling), device_id_type=MESH
    )
    xw.start()
    swaps = []
    for i in range(HALF):
        other = (1 - core) * HALF + i
        kc = pltpu.make_async_remote_copy(
            k_hbm.at[:, cols(other)], k_buf.at[1, i], xk_send.at[i], xk_recv.at[i],
            device_id=(group, sibling), device_id_type=MESH,
        )
        vc = pltpu.make_async_remote_copy(
            v_hbm.at[:, cols(other)], v_buf.at[1, i], xv_send.at[i], xv_recv.at[i],
            device_id=(group, sibling), device_id_type=MESH,
        )
        kc.start()
        vc.start()
        swaps.append((kc, vc))
    q_loads = []
    for slot in range(HEADS):
        qc = pltpu.make_async_copy(q_hbm.at[:, cols(own_head(slot))], q_buf.at[slot], q_sem.at[slot])
        qc.start()
        q_loads.append(qc)

    def local_state(c):
        for copy in loads[c]:
            copy.wait()
        if c == 0:
            xw.wait_recv()
        for copy in swaps[c]:
            copy.wait_recv()
        kt[0] = k_buf[0, c].T
        kt[1] = k_buf[1, c].T

        def one(m, carry):
            own = kt[0] * own_w[pl.ds(m, 1), :].astype(jnp.bfloat16)
            sib = kt[1] * sib_w[pl.ds(m, 1), :].astype(jnp.bfloat16)
            total = jnp.dot(own, v_buf[0, c], preferred_element_type=jnp.float32)
            total += jnp.dot(sib, v_buf[1, c], preferred_element_type=jnp.float32)
            st[c, pl.ds(pl.multiple_of(m * HDIM, HDIM), HDIM), :] = total
            return carry

        lax.fori_loop(0, MEMS, one, 0, unroll=4)

    low = [0] * HALF
    lows = [[] for _ in range(HALF)]
    reduces = [[] for _ in range(HALF)]
    gathers = [dict() for _ in range(HALF)]

    def rows(start, size):
        return pl.ds(pl.multiple_of(start, size), size)

    def part(start, size):
        if size >= HDIM:
            return (pl.ds(start // HDIM, size // HDIM),)
        return (start // HDIM, rows(start % HDIM, size))

    def send_half(c, s):
        size = ROWS >> (s + 1)
        b = bit(orders[c][s])
        lows[c].append(low[c])
        away = rows(low[c] + (1 - b) * size, size)
        low[c] = low[c] + b * size
        sbuf[c, away, :] = st[c, away, :].astype(jnp.bfloat16)
        copy = pltpu.make_async_remote_copy(
            sbuf.at[c, away], rbuf.at[c, size : 2 * size],
            r_send.at[c, s], r_recv.at[c, s],
            device_id=partner(orders[c][s]), device_id_type=MESH,
        )
        copy.start()
        reduces[c].append(copy)

    def gather(c, s):
        size = ROWS >> (s + 1)
        b = bit(orders[c][s])
        have = part(lows[c][s] + b * size, size)
        copy = pltpu.make_async_remote_copy(
            sh[c].at[*have], sh[c].at[*have],
            g_send.at[c, s], g_recv.at[c, s],
            device_id=partner(orders[c][s]), device_id_type=MESH,
        )
        copy.start()
        gathers[c][s] = copy

    cores = {}
    outs = []

    def readout(slot):
        q_loads[slot].wait()
        head = own_head(slot)
        scale = gain_buf[pl.ds(head, 1), :]

        def one(g, carry):
            for b in range(GROUP):
                b = g * GROUP + b
                here = pl.ds(pl.multiple_of(b * BLOCK, BLOCK), BLOCK)
                pair = jnp.concatenate(
                    [
                        sh[slot][ids[r, b]]
                        for r in range(2)
                    ],
                    axis=1,
                )
                product = jnp.dot(q_buf[slot, here, :], pair, preferred_element_type=jnp.float32)
                gates = [levels[r, b].astype(jnp.float32) / GATE_DEN for r in range(2)]
                total = gates[0] * product[:, :HDIM] + gates[1] * product[:, HDIM:]
                square = jnp.mean(total * total, axis=-1, keepdims=True)
                result = total * lax.rsqrt(square + 1e-05) * scale
                o_buf[slot, here, :] = result.astype(jnp.bfloat16)
            return carry

        lax.fori_loop(0, blocks // GROUP, one, 0)
        copy = pltpu.make_async_copy(o_buf.at[slot], o_hbm.at[:, cols(head)], o_sem.at[slot])
        copy.start()
        outs.append(copy)

    def stage(c, k):
        if k == 0:
            local_state(c)
            send_half(c, 0)
        elif k <= steps:
            s = k - 1
            size = ROWS >> (s + 1)
            reduces[c][s].wait_recv()
            keep = rows(low[c], size)
            total = st[c, keep, :] + rbuf[c, size : 2 * size, :].astype(jnp.float32)
            if k < steps:
                st[c, keep, :] = total
                send_half(c, k)
            else:
                owned = total.astype(jnp.bfloat16)
                if size >= HDIM:
                    owned = owned.reshape(size // HDIM, HDIM, HDIM)
                sh[c][part(low[c], size)] = owned
                gather(c, steps - 1)
        elif k < 2 * steps:
            s = 2 * steps - k
            gathers[c][s].wait_recv()
            gather(c, s - 1)
        elif k == 2 * steps:
            gathers[c][0].wait_recv()
            copy = pltpu.make_async_remote_copy(
                sh[c], sh[HALF + c], c_send.at[c], c_recv.at[c],
                device_id=(group, sibling), device_id_type=MESH,
            )
            copy.start()
            cores[c] = copy
            readout(c)
        else:
            cores[c].wait_recv()
            readout(HALF + c)

    plan = [(c + LAG * k, -k, c) for c in range(HALF) for k in range(2 * steps + 2)]
    for _, k, c in sorted(plan):
        stage(c, -k)

    xw.wait_send()
    for i in range(HALF):
        swaps[i][0].wait_send()
        swaps[i][1].wait_send()
        cores[i].wait_send()
        for s in range(steps):
            reduces[i][s].wait_send()
            gathers[i][s].wait_send()
    for copy in outs:
        copy.wait()


def plan_kernel(
    tok, chunks, order_end, order_inner,
    q_hbm, k_hbm, v_hbm, ids_hbm, levels_hbm, gain,
    out,
    ids, levels, sib_ids, sib_levels, q_buf, k_buf, v_buf, own_w, sib_w, kt, st, sbuf, ybuf, zbuf, mbuf,
    sh0, sh1, sh2, sh3, sh4, sh5, sh6, sh7, sh8, sh9, sh10, sh11, sh12, sh13, sh14, sh15,
    gain_buf, q_sem, k_sem, v_sem, n_sem,
    xk_send, xk_recv, xv_send, xv_recv, xw_send, xw_recv,
    c_send, c_recv, p_send, p_recv,
):
    sh = (sh0, sh1, sh2, sh3, sh4, sh5, sh6, sh7, sh8, sh9, sh10, sh11, sh12, sh13, sh14, sh15)
    group = lax.axis_index("groups")
    me = lax.axis_index("seq")
    core = me % 2
    y = (me // 2) % 2
    z = me // 4
    high = z // 2
    inner = (z + high) % 2
    sibling = me + 1 - 2 * core
    towards = {
        "y": me + 2 - 4 * y,
        "s": me + 4 - 8 * (z % 2),
        "m": me + 4 * (3 - 2 * z),
    }

    def device(way):
        return (group, towards[way])

    def cols(head):
        return pl.ds(pl.multiple_of(head * HDIM, HDIM), HDIM)

    def own_head(slot):
        return core * HALF + slot if slot < HALF else (1 - core) * HALF + slot - HALF

    barrier = pltpu.get_barrier_semaphore()
    pl.semaphore_signal(barrier, inc=1, device_id=(group, sibling), device_id_type=MESH)
    pl.semaphore_signal(barrier, inc=1, device_id=device("y"), device_id_type=MESH)
    pl.semaphore_signal(barrier, inc=1, device_id=device("s"), device_id_type=MESH)

    @pl.when(inner == 1)
    def _():
        pl.semaphore_signal(barrier, inc=1, device_id=device("m"), device_id_type=MESH)

    loads = []
    swaps = []
    q_loads = []
    for i in range(HALF):
        mine, other = cols(own_head(i)), cols((1 - core) * HALF + i)
        pairs = ((k_hbm, k_buf, k_sem, xk_send, xk_recv), (v_hbm, v_buf, v_sem, xv_send, xv_recv))
        loads.append([
            pltpu.make_async_copy(hbm.at[:, mine], buf.at[0, i], sem.at[i])
            for hbm, buf, sem, _, _ in pairs
        ])
        swaps.append([
            pltpu.make_async_remote_copy(
                hbm.at[:, other], buf.at[1, i], send.at[i], recv.at[i],
                device_id=(group, sibling), device_id_type=MESH,
            )
            for hbm, buf, _, send, recv in pairs
        ])
    for slot in range(HEADS):
        q_loads.append(
            pltpu.make_async_copy(q_hbm.at[:, cols(own_head(slot))], q_buf.at[slot], q_sem.at[slot])
        )

    def start(copies):
        for copy in copies:
            copy.start()

    small = [
        pltpu.make_async_copy(ids_hbm, ids, n_sem.at[0]),
        pltpu.make_async_copy(levels_hbm, levels, n_sem.at[1]),
        pltpu.make_async_copy(gain, gain_buf, n_sem.at[2]),
    ]

    start(small)
    start(loads[0])
    pl.semaphore_wait(barrier, 3 + inner)
    lists = [
        pltpu.make_async_remote_copy(
            hbm, there, xw_send.at[i], xw_recv.at[i],
            device_id=(group, sibling), device_id_type=MESH,
        )
        for i, (hbm, there) in enumerate(((ids_hbm, sib_ids), (levels_hbm, sib_levels)))
    ]
    start(lists)
    start(swaps[0])
    for i in range(1, AHEAD):
        start(loads[i])
        start(swaps[i])

    blocks = tok // BLOCK
    member = lax.broadcasted_iota(jnp.int32, (MEMS, 2 * BLOCK), 0)
    lane = lax.broadcasted_iota(jnp.int32, (MEMS, 2 * BLOCK), 1)

    def weigh(to, names, amounts):
        for p in range(blocks // 2):
            w = []
            for b in (2 * p, 2 * p + 1):
                w.append(
                    jnp.where(member == names[0, b], amounts[0, b], 0)
                    + jnp.where(member == names[1, b], amounts[1, b], 0)
                )
            both = jnp.where(lane < BLOCK, w[0], w[1]).astype(jnp.float32) / GATE_DEN
            to[:, p * 2 * BLOCK : (p + 1) * 2 * BLOCK] = both

    for copy in small:
        copy.wait()
    weigh(own_w, ids, levels)
    for copy in lists:
        copy.wait_recv()
    weigh(sib_w, sib_ids, sib_levels)

    fetched = set()
    asked = set()

    def fetch(c):
        if c in fetched:
            return
        for copy in loads[c]:
            copy.wait()
        fetched.add(c)
        kt[0] = k_buf[0, c].T
        for copy in swaps[c]:
            copy.wait_recv()
        if c + AHEAD < HALF:
            start(loads[c + AHEAD])
            start(swaps[c + AHEAD])
        kt[1] = k_buf[1, c].T

    def ask(c):
        if c not in asked:
            asked.add(c)
            start([q_loads[c], q_loads[HALF + c]])

    def local(c, first, count):
        for i in range(count):
            m = first + i
            own = kt[0] * own_w[pl.ds(m, 1), :].astype(jnp.bfloat16)
            sib = kt[1] * sib_w[pl.ds(m, 1), :].astype(jnp.bfloat16)
            total = jnp.dot(own, v_buf[0, c], preferred_element_type=jnp.float32)
            total += jnp.dot(sib, v_buf[1, c], preferred_element_type=jnp.float32)
            st[c, mem_rows(m, 1), :] = total

    def mem_rows(m, count):
        return pl.ds(pl.multiple_of(m * HDIM, HDIM), count * HDIM)

    landing = {"y": ybuf, "s": zbuf, "m": mbuf}

    def reduce_copy(k, way, m, count):
        c = chunks[k][0]
        slot = TAGS.index("r") * len(WAYS) + WAYS.index(way)
        return pltpu.make_async_remote_copy(
            sbuf.at[c, mem_rows(m, count)], landing[way].at[c, mem_rows(m, count)],
            p_send.at[k, slot], p_recv.at[k, slot], device_id=device(way), device_id_type=MESH,
        )

    def gather_copy(k, way, tag, m, count):
        c = chunks[k][0]
        slot = TAGS.index(tag) * len(WAYS) + WAYS.index(way)
        here = sh[c].at[pl.ds(m, count)]
        return pltpu.make_async_remote_copy(
            here, here, p_send.at[k, slot], p_recv.at[k, slot],
            device_id=device(way), device_id_type=MESH,
        )

    def run(order, end):
        sent = []
        fetched.clear()
        asked.clear()

        def give(k, way, m, count):
            c = chunks[k][0]
            copy = reduce_copy(k, way, m, count)
            copy.start()
            sent.append(copy)

        def pack(k, m, count):
            c = chunks[k][0]
            here = mem_rows(m, count)
            sbuf[c, here, :] = st[c, here, :].astype(jnp.bfloat16)

        def total(k, ways, m, count):
            c = chunks[k][0]
            here = mem_rows(m, count)
            value = st[c, here, :]
            for way in ways:
                value = value + landing[way][c, here, :].astype(jnp.float32)
            return value

        def forward(k, ways, m, count, ways_sum):
            c = chunks[k][0]
            sbuf[c, mem_rows(m, count), :] = total(k, ways_sum, m, count).astype(jnp.bfloat16)
            give(k, ways, m, count)

        def finish(k, ways_sum, m, count):
            c = chunks[k][0]
            value = total(k, ways_sum, m, count).astype(jnp.bfloat16)
            sh[c][pl.ds(m, count)] = value.reshape(count, HDIM, HDIM)

        def share(k, way, tag, m, count):
            copy = gather_copy(k, way, tag, m, count)
            copy.start()
            sent.append(copy)

        def got(k, way, m, count):
            reduce_copy(k, way, m, count).wait_recv()

        def have(k, way, tag, m, count):
            gather_copy(k, way, tag, m, count).wait_recv()

        def readout(slot):
            q_loads[slot].wait()
            head = own_head(slot)
            scale = gain_buf[pl.ds(head, 1), :]
            for b in range(blocks):
                here = pl.ds(b * BLOCK, BLOCK)
                pair = jnp.concatenate([sh[slot][ids[r, b]] for r in range(2)], axis=1)
                product = jnp.dot(q_buf[slot, here, :], pair, preferred_element_type=jnp.float32)
                gates = [levels[r, b].astype(jnp.float32) / GATE_DEN for r in range(2)]
                value = gates[0] * product[:, :HDIM] + gates[1] * product[:, HDIM:]
                square = jnp.mean(value * value, axis=-1, keepdims=True)
                result = value * lax.rsqrt(square + 1e-05) * scale
                out[here, cols(head)] = result.astype(jnp.bfloat16)

        def cross(c):
            return pltpu.make_async_remote_copy(
                sh[c], sh[HALF + c], c_send.at[c], c_recv.at[c],
                device_id=(group, sibling), device_id_type=MESH,
            )

        def stage(k, s):
            c, base, u, kind = chunks[k]
            if s == 10:
                cross(c).start()
                readout(c)
                return
            if s == 11:
                cross(c).wait_recv()
                readout(HALF + c)
                return
            if kind[0] == "Y":
                mine, away = base + y * 2 * u, base + (1 - y) * 2 * u
                near, far = mine + high * u, mine + (1 - high) * u
                near2, far2 = away + high * u, away + (1 - high) * u
                if s == 0:
                    fetch(c)
                    local(c, away, 2 * u)
                    pack(k, away, 2 * u)
                    give(k, "y", away, 2 * u)
                    local(c, mine, 2 * u)
                    ask(c)
                elif s == 1:
                    got(k, "y", mine, 2 * u)
                    here = mem_rows(mine, 2 * u)
                    if end and kind == "YM":
                        forward(k, "s", mine, 2 * u, ("y",))
                    elif end:
                        forward(k, "s", far, u, ("y",))
                elif s == 2:
                    got(k, "s", mine if kind == "YM" else far, 2 * u if kind == "YM" else u)
                    forward(k, "m", far, u, ("y", "s"))
                elif s == 3:
                    got(k, "m", near, u)
                    if kind == "YE":
                        forward(k, "s", near, u, ("y", "m"))
                    else:
                        finish(k, ("y", "s", "m"), near, u)
                        share(k, "m", "n", near, u)
                        share(k, "s", "n", near, u)
                        share(k, "y", "n", near, u)
                elif s == 4:
                    got(k, "s", near, u)
                    finish(k, ("y", "s"), near, u)
                    share(k, "s", "n", near, u)
                    share(k, "y", "n", near, u)
                elif s == 5:
                    if kind == "YE":
                        have(k, "s", "n", near, u)
                        share(k, "m", "n", near, u)
                        share(k, "y", "n", near, u)
                    else:
                        have(k, "m", "n", far, u)
                        share(k, "s", "f", far, u)
                        share(k, "y", "f", far, u)
                elif s == 6:
                    if end:
                        have(k, "s", "n", near, u)
                        share(k, "y", "n", near, u)
                    else:
                        have(k, "m", "n", far, u)
                        share(k, "s", "f", far, u)
                        share(k, "y", "f", far, u)
                elif s == 7:
                    have(k, "s", "f", far, u)
                    share(k, "y", "f", far, u)
                elif s == 8:
                    have(k, "y", "n", near2, u)
                    have(k, "y", "f", far2, u)
            else:
                near, far = base + high * 2 * u, base + (1 - high) * 2 * u
                mine, away = near + y * u, near + (1 - y) * u
                mine2, away2 = far + y * u, far + (1 - y) * u
                if s == 0:
                    fetch(c)
                    local(c, far, 2 * u)
                    if end and kind == "ZE":
                        pack(k, far, 2 * u)
                        give(k, "s", far, 2 * u)
                    local(c, near, 2 * u)
                    if end and kind == "ZM":
                        pack(k, base, 4 * u)
                        give(k, "s", base, 4 * u)
                    ask(c)
                elif kind == "ZE":
                    if s == 1:
                        got(k, "s", far, 2 * u)
                        forward(k, "m", far, 2 * u, ("s",))
                    elif s == 2:
                        got(k, "m", near, 2 * u)
                        forward(k, "s", near, 2 * u, ("m",))
                    elif s == 3 and end:
                        got(k, "s", near, 2 * u)
                        forward(k, "y", away, u, ("s",))
                    elif s == 4 and end:
                        got(k, "y", mine, u)
                        finish(k, ("s", "y"), mine, u)
                        share(k, "y", "n", mine, u)
                        share(k, "s", "n", mine, u)
                    elif s == 5 and end:
                        have(k, "y", "n", away, u)
                        share(k, "s", "f", away, u)
                    elif s == 4:
                        have(k, "s", "n", mine, u)
                        share(k, "m", "n", mine, u)
                    elif s == 5:
                        have(k, "s", "f", away, u)
                        share(k, "m", "f", away, u)
                    elif s == 6:
                        have(k, "m", "n", mine2, u)
                        share(k, "s", "h", mine2, u)
                    elif s == 7 and not end:
                        have(k, "m", "f", away2, u)
                        share(k, "s", "i", away2, u)
                    elif s == 7:
                        have(k, "s", "h", mine2, u)
                    elif s == 8 and end:
                        have(k, "s", "i", away2, u)
                else:
                    if s == 1:
                        got(k, "s", base, 4 * u)
                        forward(k, "m", far, 2 * u, ("s",))
                    elif s == 2:
                        got(k, "m", near, 2 * u)
                        forward(k, "y", away, u, ("s", "m"))
                    elif s == 3:
                        got(k, "y", mine, u)
                        finish(k, ("s", "m", "y"), mine, u)
                        share(k, "y", "n", mine, u)
                        share(k, "m", "n", mine, u)
                        share(k, "s", "n", mine, u)
                    elif s == 4:
                        have(k, "y", "n", away, u)
                        share(k, "m", "f", away, u)
                        share(k, "s", "f", away, u)
                    elif s == 5:
                        have(k, "m", "n", mine2, u)
                        share(k, "s", "h", mine2, u)
                    elif s == 6 and not end:
                        have(k, "m", "f", away2, u)
                        share(k, "s", "i", away2, u)
                    elif s == 6:
                        have(k, "s", "n", mine, u)
                    elif s == 7 and end:
                        have(k, "s", "f", away, u)
                    elif s == 8 and end:
                        have(k, "s", "h", mine2, u)
                        have(k, "s", "i", away2, u)

        for k, s in order:
            stage(k, s)
        for copy in sent:
            copy.wait_send()
        for c in range(HALF):
            cross(c).wait_send()

    @pl.when(inner == 0)
    def _():
        run(order_end, True)

    @pl.when(inner == 1)
    def _():
        run(order_inner, False)

    for copy in lists:
        copy.wait_send()
    for i in range(HALF):
        swaps[i][0].wait_send()
        swaps[i][1].wait_send()


def body(n, queries, keys, values, memory_ids, gate_levels, norm_gain):
    tok = queries.shape[0]
    masks = []
    mask = 2
    while mask < n:
        masks.append(mask)
        mask *= 2
    plain = tuple(masks)
    turned = (masks[1], masks[0]) + tuple(masks[2:])
    orders = [turned if c % 4 == 2 else plain for c in range(HALF)]
    steps = len(masks)
    bf = jnp.bfloat16
    dma = pltpu.SemaphoreType.DMA
    hbm = pl.BlockSpec(memory_space=pl.ANY)
    smem = pl.BlockSpec(memory_space=pltpu.SMEM)
    return pl.pallas_call(
        functools.partial(kernel, n, tok, orders),
        out_shape=jax.ShapeDtypeStruct((tok, HEADS * HDIM), bf),
        in_specs=[hbm, hbm, hbm, smem, smem, hbm],
        out_specs=hbm,
        scratch_shapes=[
            pltpu.VMEM((HEADS, tok, HDIM), bf),
            pltpu.VMEM((2, HALF, tok, HDIM), bf),
            pltpu.VMEM((2, HALF, tok, HDIM), bf),
            pltpu.VMEM((HEADS, tok, HDIM), bf),
            pltpu.VMEM((MEMS, tok), jnp.float32),
            pltpu.VMEM((MEMS, tok), jnp.float32),
            pltpu.VMEM((2, HDIM, tok), bf),
            pltpu.VMEM((HALF, ROWS, HDIM), jnp.float32),
            pltpu.VMEM((HALF, ROWS, HDIM), bf),
            pltpu.VMEM((HALF, ROWS, HDIM), bf),
            *[pltpu.VMEM((MEMS, HDIM, HDIM), bf) for _ in range(HEADS)],
            pltpu.VMEM((HEADS, HDIM), jnp.float32),
            dma((HEADS,)), dma((HALF,)), dma((HALF,)), dma((HEADS,)), dma((1,)),
            dma((HALF,)), dma((HALF,)), dma((HALF,)), dma((HALF,)), dma((1,)), dma((1,)),
            dma((HALF,)), dma((HALF,)),
            dma((HALF, steps)), dma((HALF, steps)), dma((HALF, steps)), dma((HALF, steps)),
        ],
        compiler_params=pltpu.CompilerParams(
            collective_id=0, has_side_effects=True, vmem_limit_bytes=48 * 1024 * 1024
        ),
        name="memory_readout",
    )(queries, keys, values, memory_ids.T, gate_levels.T, norm_gain.reshape(HEADS, HDIM))


def planned_body(queries, keys, values, memory_ids, gate_levels, norm_gain):
    tok = queries.shape[0]
    bf = jnp.bfloat16
    dma = pltpu.SemaphoreType.DMA
    hbm = pl.BlockSpec(memory_space=pltpu.HBM)
    kinds = len(TAGS) * len(WAYS)
    return pl.pallas_call(
        functools.partial(plan_kernel, tok, CHUNKS, ORDER_END, ORDER_INNER),
        out_shape=jax.ShapeDtypeStruct((tok, HEADS * HDIM), bf),
        in_specs=[hbm] * 6,
        out_specs=pl.BlockSpec(memory_space=pltpu.VMEM),
        scratch_shapes=[
            *[pltpu.SMEM((2, tok // BLOCK), jnp.int32) for _ in range(4)],
            pltpu.VMEM((HEADS, tok, HDIM), bf),
            pltpu.VMEM((2, HALF, tok, HDIM), bf),
            pltpu.VMEM((2, HALF, tok, HDIM), bf),
            pltpu.VMEM((MEMS, tok), jnp.float32),
            pltpu.VMEM((MEMS, tok), jnp.float32),
            pltpu.VMEM((2, HDIM, tok), bf),
            pltpu.VMEM((HALF, ROWS, HDIM), jnp.float32),
            *[pltpu.VMEM((HALF, ROWS, HDIM), bf) for _ in range(4)],
            *[pltpu.VMEM((MEMS, HDIM, HDIM), bf) for _ in range(HEADS)],
            pltpu.VMEM((HEADS, HDIM), jnp.float32),
            dma((HEADS,)), dma((HALF,)), dma((HALF,)), dma((3,)),
            dma((HALF,)), dma((HALF,)), dma((HALF,)), dma((HALF,)), dma((2,)), dma((2,)),
            dma((HALF,)), dma((HALF,)),
            dma((len(CHUNKS), kinds)), dma((len(CHUNKS), kinds)),
        ],
        compiler_params=pltpu.CompilerParams(
            collective_id=0, has_side_effects=True, vmem_limit_bytes=48 * 1024 * 1024
        ),
        name="memory_readout",
    )(queries, keys, values, memory_ids.T, gate_levels.T, norm_gain.reshape(HEADS, HDIM))


def solution(mesh):
    rows = P(("groups", "seq"), None)
    n = mesh.shape["seq"]
    part = planned_body if n == PLANNED else functools.partial(body, n)
    return jax.shard_map(
        part,
        mesh=mesh,
        in_specs=(rows, rows, rows, rows, rows, P()),
        out_specs=rows,
        check_vma=False,
    )
```
